256 devices in a mesh: row: 64 (over x, z_hi, y), col: 4 (over z_lo, core).
Axes of the slice: x: 4, y: 4, z: 8 (z_hi: 4, z_lo: 2; z = z_hi * 2 + z_lo), core: 2. Of those that a mesh axis runs over, the one named last changes fastest.
Arguments:
- features: bfloat16 [512, 512, 256], P('row', 'col'), may hold values from -6 to 6
- target: bfloat16 [512, 512, 256], P('row', 'col'), may hold values from -6 to 6
- hole_mask: int32 [512, 512], P('row', 'col'), may hold values 0 or 1
- kernel_first: bfloat16 [3, 3, 256, 256], replicated, may hold values from -0.125 to 0.125
- kernel_second: bfloat16 [3, 3, 256, 256], replicated, may hold values from -0.125 to 0.125
- inputs: bfloat16 [512, 512, 512], P(('row', 'col')), may hold values from -6 to 6
- weight_in: bfloat16 [512, 192], replicated, may hold values from -0.25 to 0.25
- weight_out: bfloat16 [192, 256], replicated, may hold values from -0.4375 to 0.4375
- weight_local: bfloat16 [512, 256], replicated, may hold values from -0.25 to 0.25
- weight_mix: bfloat16 [384, 384], replicated, may hold values from -0.3125 to 0.3125
Outputs:
- grad_inputs: bfloat16 [512, 512, 512], P(('row', 'col'))
The draws below stay inside these ranges and needn't reach their ends.
Inputs may be any that keep to these rules, and one draw needn't show every extreme that they name: `hole_mask`: 1 marks a pixel to be filled.
All inputs are finite; a program needn't handle non-finite values. No bound on the sum of `hole_mask` on one device may be relied on, other than what follows from the above.
Results may differ from the reference program's by a relative error of at most 0.0095.
Values may be sent and summed in bfloat16 or wider, within the bound.
A program may use at most 64 MiB of HBM per device.

```python
import math
import jax
import jax.numpy as jnp
from jax import lax

C1 = 256
CF = 512
S = 192
H = 512
W = 512


def set_ends(result, key, smallest, high):
    longest = result.shape.index(max(result.shape))
    spots = []
    for shift in (0, 1):
        where = [jax.random.randint(jax.random.fold_in(key, axis), (), 0, length) for axis, length in enumerate(result.shape)]
        where[longest] = (where[longest] + shift) % result.shape[longest]
        spots.append(tuple(where))
    return result.at[spots[0]].set(smallest).at[spots[1]].set(high)


def level_of(key, shape, cuts, low, largest):
    factor_of, own = 1.0, jax.random.fold_in(key, 6)
    for dim, shards_of in cuts:
        draws = jnp.exp(jax.random.uniform(jax.random.fold_in(own, dim), (shards_of,), jnp.float32, low / len(cuts), largest / len(cuts)))
        factor_of = factor_of * jnp.repeat(draws, shape[dim] // shards_of).reshape([-1 if axis == dim else 1 for axis in range(len(shape))])
    return factor_of


def noise(stream_key, extent, deviation, most, pieces=(), held_as=jnp.bfloat16):
    level = level_of(stream_key, extent, pieces, -0.22, 0.18) if pieces else 1.0
    values = jax.random.normal(stream_key, extent, jnp.float32) * deviation * level
    return jnp.minimum(jnp.maximum(values, -most), most).astype(held_as)


def setup_inputs(seed: int = 0) -> dict:
    splits = jax.random.split(jax.random.key(seed), 11)
    return {
        "features": noise(splits[0], (H, W, C1), 1.0, 6.0, ((0, 64), (1, 4))),
        "target": noise(splits[1], (H, W, C1), 1.0, 6.0, ((0, 64), (1, 4))),
        "hole_mask": set_ends((jax.random.randint(splits[2], (H, W), 0, 2) < 1).astype(jnp.int32), jax.random.fold_in(splits[2], 1), 0, 1),
        "kernel_first": noise(splits[3], (3, 3, C1, C1), (9 * C1) ** -0.5, 0.125),
        "kernel_second": noise(splits[4], (3, 3, C1, C1), (9 * C1) ** -0.5, 0.125),
        "inputs": noise(splits[5], (H, W, CF), 1.0, 6.0, ((0, 256),)),
        "weight_in": noise(splits[6], (CF, S), CF ** -0.5, 0.25),
        "weight_out": noise(splits[7], (S, C1), S ** -0.5, 0.4375),
        "weight_local": noise(splits[8], (CF, C1), CF ** -0.5, 0.25),
        "weight_mix": noise(splits[9], (2 * S, 2 * S), (2 * S) ** -0.5, 0.3125),
    }


def conv_valid(padded, kernel):
    output = lax.conv_general_dilated(padded[None].astype(jnp.float32), kernel.astype(jnp.float32), (1, 1), 'VALID', rhs_dilation=(2, 2), dimension_numbers=('NHWC', 'HWIO', 'NHWC'))
    return output[0]

def same_conv(signal, kernel):
    padded = jnp.pad(signal, ((2, 2), (2, 2), (0, 0)))
    return conv_valid(padded, kernel)

def adjoint_kernel(kernel):
    return jnp.transpose(jnp.flip(kernel, (0, 1)), (0, 1, 3, 2))

def silu_slope(pre_value):
    sigmoid_value = jax.nn.sigmoid(pre_value)
    return sigmoid_value * (1.0 + pre_value * (1.0 - sigmoid_value))

def dft_tables(first_ids, second_ids, length):
    phases = first_ids[:, None] * second_ids[None, :] % length
    angles = phases.astype(jnp.float32) * (2.0 * math.pi / length)
    return (jnp.cos(angles).astype(jnp.bfloat16), jnp.sin(angles).astype(jnp.bfloat16))

def column_tables(grid_width):
    freq_ids = jnp.arange(grid_width // 2, dtype=jnp.int32)
    col_ids = jnp.arange(grid_width, dtype=jnp.int32)
    cos_table, sin_table = dft_tables(freq_ids, col_ids, grid_width)
    alternate = (2 * (col_ids % 2) - 1).astype(jnp.float32).astype(jnp.bfloat16)
    sin_table = jnp.where((freq_ids == 0)[:, None], alternate[None, :], sin_table)
    return (cos_table, sin_table)

def column_transform(signal, cos_table, sin_table, norm_factor):
    cosine_part = jnp.einsum('rws,kw->rks', signal.astype(jnp.float32), cos_table.astype(jnp.float32))
    sine_part = jnp.einsum('rws,kw->rks', signal.astype(jnp.float32), sin_table.astype(jnp.float32))
    return (jnp.concatenate([cosine_part, -sine_part], axis=-1) * norm_factor).astype(jnp.bfloat16)

def row_forward(spectrum, cos_table, sin_table, norm_factor, half_width):
    cosine_part = jnp.einsum('kp,pmc->kmc', cos_table.astype(jnp.float32), spectrum.astype(jnp.float32))
    sine_part = jnp.einsum('kp,pmc->kmc', sin_table.astype(jnp.float32), spectrum.astype(jnp.float32))
    real_part = cosine_part[..., :half_width] + sine_part[..., half_width:]
    imag_part = cosine_part[..., half_width:] - sine_part[..., :half_width]
    return jnp.concatenate([real_part, imag_part], axis=-1) * norm_factor

def row_inverse(spectrum, cos_table, sin_table, norm_factor, half_width):
    cosine_part = jnp.einsum('kp,kmc->pmc', cos_table.astype(jnp.float32), spectrum.astype(jnp.float32))
    sine_part = jnp.einsum('kp,kmc->pmc', sin_table.astype(jnp.float32), spectrum.astype(jnp.float32))
    real_part = cosine_part[..., :half_width] - sine_part[..., half_width:]
    imag_part = cosine_part[..., half_width:] + sine_part[..., :half_width]
    return (jnp.concatenate([real_part, imag_part], axis=-1) * norm_factor).astype(jnp.bfloat16)

def column_inverse(spectrum, cos_table, sin_table, norm_factor, half_width):
    cosine_part = jnp.einsum('rks,kw->rws', spectrum[..., :half_width].astype(jnp.float32), cos_table.astype(jnp.float32))
    sine_part = jnp.einsum('rks,kw->rws', spectrum[..., half_width:].astype(jnp.float32), sin_table.astype(jnp.float32))
    return ((cosine_part - sine_part) * norm_factor).astype(jnp.bfloat16)

def reference(features, target, hole_mask, kernel_first, kernel_second, inputs, weight_in, weight_out, weight_local, weight_mix):
    pre_first = same_conv(features, kernel_first)
    act_first = jax.nn.silu(pre_first).astype(jnp.bfloat16)
    pre_second = same_conv(act_first, kernel_second)
    hole_weight = 1.0 + 2.0 * hole_mask.astype(jnp.float32)
    loss_grad = (hole_weight[:, :, None] * (pre_second - target.astype(jnp.float32))).astype(jnp.bfloat16)
    grad_act = same_conv(loss_grad, adjoint_kernel(kernel_second))
    grad_pre = (grad_act * silu_slope(pre_first)).astype(jnp.bfloat16)
    grad_feat = same_conv(grad_pre, adjoint_kernel(kernel_first)).astype(jnp.bfloat16)
    spatial = jnp.einsum('rwf,fs->rws', inputs.astype(jnp.float32), weight_in.astype(jnp.float32)).astype(jnp.bfloat16)
    grad_spec = jnp.einsum('rwc,sc->rws', grad_feat.astype(jnp.float32), weight_out.astype(jnp.float32)).astype(jnp.bfloat16)
    grad_local = jnp.einsum('rwc,fc->rwf', grad_feat.astype(jnp.float32), weight_local.astype(jnp.float32))
    row_ids = jnp.arange(H, dtype=jnp.int32)
    cos_cols, sin_cols = column_tables(W)
    cos_rows, sin_rows = dft_tables(row_ids, row_ids, H)
    col_factor = 1.0 / math.sqrt(W)
    row_factor = 1.0 / math.sqrt(H)
    spatial_cols = column_transform(spatial, cos_cols, sin_cols, col_factor)
    grad_cols = column_transform(grad_spec, cos_cols, sin_cols, col_factor)
    spatial_freq = row_forward(spatial_cols, cos_rows, sin_rows, row_factor, S)
    grad_freq = row_forward(grad_cols, cos_rows, sin_rows, row_factor, S)
    pre_mix = jnp.einsum('kmc,cd->kmd', spatial_freq.astype(jnp.bfloat16).astype(jnp.float32), weight_mix.astype(jnp.float32))
    grad_mix = (grad_freq * silu_slope(pre_mix)).astype(jnp.bfloat16)
    grad_back = jnp.einsum('kmd,cd->kmc', grad_mix.astype(jnp.float32), weight_mix.astype(jnp.float32)).astype(jnp.bfloat16)
    grad_rows = row_inverse(grad_back, cos_rows, sin_rows, row_factor, S)
    grad_spatial = column_inverse(grad_rows, cos_cols, sin_cols, col_factor, S)
    grad_total = jnp.einsum('rws,fs->rwf', grad_spatial.astype(jnp.float32), weight_in.astype(jnp.float32)) + grad_local
    return grad_total.astype(jnp.bfloat16)
```

```python
import functools
import math

import jax
import jax.numpy as jnp
import numpy as np
from jax import lax
from jax.experimental import pallas as pl
from jax.experimental.pallas import tpu as pltpu
from jax.sharding import PartitionSpec as P

def padded_2(shard, sides, width):
    for axis, dim in sides:
        size, length = (lax.axis_size(axis), shard.shape[dim])
        up = [(i, (i + 1) % size) for i in range(size - 1)]
        down = [(j, i) for i, j in up]
        last = lax.slice_in_dim(shard, length - width, length, axis=dim)
        initial = lax.slice_in_dim(shard, 0, width, axis=dim)
        before = lax.ppermute(last, axis, up)
        after = lax.ppermute(initial, axis, down)
        shard = jnp.concatenate([before, shard, after], axis=dim)
    return shard


def conv_valid(padded, kernel):
    output = lax.conv_general_dilated(
        padded[None],
        kernel,
        (1, 1),
        "VALID",
        rhs_dilation=(2, 2),
        dimension_numbers=("NHWC", "HWIO", "NHWC"),
        preferred_element_type=jnp.float32,
    )
    return output[0]


def adjoint_kernel(kernel):
    return jnp.transpose(jnp.flip(kernel, (0, 1)), (0, 1, 3, 2))


def silu_slope(pre_value):
    sigmoid_value = jax.nn.sigmoid(pre_value)
    return sigmoid_value * (1.0 + pre_value * (1.0 - sigmoid_value))


MESH = pl.DeviceIdType.MESH


def host_tables(length):
    ids = np.arange(length, dtype=np.int64)
    angles = (2.0 * np.pi / length) * ((ids[:, None] * ids[None, :]) % length)
    return (np.cos(angles).astype(jnp.bfloat16), np.sin(angles).astype(jnp.bfloat16))


def duplicated(weight):
    depth, width = weight.shape
    chunks = weight.reshape(depth, width // 64, 1, 64)
    return jnp.broadcast_to(chunks, (depth, width // 64, 2, 64)).reshape(depth, 2 * width)


def interleaved(weight):
    half = weight.shape[0] // 2
    parts = weight.reshape(2, half // 64, 64, 2, half // 64, 64)
    return parts.transpose(1, 0, 2, 4, 3, 5).reshape(2 * half, 2 * half)


def dot(left, right):
    return jnp.dot(left, right, preferred_element_type=jnp.float32)


def spectral_kernel(
    sizes,
    inputs_ref,
    strip_ref,
    win_ref,
    wout_ref,
    wmix_ref,
    wmix_t_ref,
    cos_ref,
    sin_ref,
    out_ref,
    spatial_out,
    spatial_in,
    grad_out,
    grad_in,
    back_out,
    back_in,
    col_cos,
    col_sin,
    col_cos_t,
    col_sin_t,
    held,
    slope_ref,
    send_sems,
    recv_sems,
):
    rows, cols, height, width, chunks = sizes
    devices = rows * cols
    lanes = chunks * 128
    me = lax.axis_index("row") * cols + lax.axis_index("col")
    barrier = pltpu.get_barrier_semaphore()

    def peer_of(step):
        return lax.rem(me + lax.rem(step * 77, devices), devices)

    def place(peer):
        return {"row": lax.div(peer, cols), "col": lax.rem(peer, cols)}

    def greet(step, carry):
        pl.semaphore_signal(barrier, inc=1, device_id=place(peer_of(step)), device_id_type=MESH)
        return carry

    lax.fori_loop(1, devices, greet, 0)
    col_factor = 1.0 / math.sqrt(width)
    row_factor = 1.0 / math.sqrt(height)
    freqs = width // 2
    pair_row = lax.broadcasted_iota(jnp.int32, (2 * freqs, freqs), 0) // 2
    pick = (pair_row == lax.broadcasted_iota(jnp.int32, (2 * freqs, freqs), 1)).astype(jnp.float32).astype(jnp.bfloat16)
    pair_col = lax.broadcasted_iota(jnp.int32, (freqs, 2 * freqs), 1) // 2
    pick_t = (pair_col == lax.broadcasted_iota(jnp.int32, (freqs, 2 * freqs), 0)).astype(jnp.float32).astype(jnp.bfloat16)
    row_id = lax.broadcasted_iota(jnp.int32, (2 * freqs, width), 0)
    alternate = (1 - 2 * (lax.broadcasted_iota(jnp.int32, (2 * freqs, width), 1) % 2)).astype(jnp.float32)
    col_cos[...] = dot(pick, cos_ref[:freqs, :]).astype(jnp.bfloat16)
    col_sin[...] = jnp.where(row_id < 2, alternate, -dot(pick, sin_ref[:freqs, :])).astype(jnp.bfloat16)
    col_id = lax.broadcasted_iota(jnp.int32, (width, 2 * freqs), 1)
    alternate_t = (1 - 2 * (lax.broadcasted_iota(jnp.int32, (width, 2 * freqs), 0) % 2)).astype(jnp.float32)
    col_cos_t[...] = dot(cos_ref[:, :freqs], pick_t).astype(jnp.bfloat16)
    col_sin_t[...] = jnp.where(col_id < 2, alternate_t, -dot(sin_ref[:, :freqs], pick_t)).astype(jnp.bfloat16)

    even_row = lax.broadcasted_iota(jnp.int32, (2 * freqs, 128), 0) % 2 == 0
    low_lane = lax.broadcasted_iota(jnp.int32, (2 * freqs, 128), 1) < 64

    def column_forward(signal_ref, weight_ref, target):
        for i in range(2):
            held[i] = dot(signal_ref[i], weight_ref[...]).astype(jnp.bfloat16)
        for j in range(chunks):
            piece = slice(j * 128, (j + 1) * 128)
            both = jnp.concatenate([held[0, :, piece], held[1, :, piece]], axis=1)
            cosine = dot(col_cos[...], both)
            sine = dot(col_sin[...], both)
            first = jnp.where(low_lane, cosine[:, :128], sine[:, :128])
            second = jnp.where(low_lane, cosine[:, 128:], sine[:, 128:])
            mixed_rows = (jnp.where(even_row, first, second) * col_factor).astype(jnp.bfloat16)
            target[j] = mixed_rows.reshape(freqs, 2, 128)

    def messages(source, target, index):
        def send(step, carry):
            peer = peer_of(step)
            pltpu.make_async_remote_copy(
                src_ref=source.at[:, peer],
                dst_ref=target.at[:, me],
                send_sem=send_sems.at[index],
                recv_sem=recv_sems.at[index],
                device_id=place(peer),
                device_id_type=MESH,
            ).start()
            return carry

        lax.fori_loop(1, devices, send, 0)
        pltpu.make_async_copy(source.at[:, me], target.at[:, me], recv_sems.at[index]).start()

    def arrived(target, index):
        pltpu.make_async_copy(target, target, recv_sems.at[index]).wait()

    def sent(source, index):
        rest = source.at[:, pl.ds(0, devices - 1)]
        pltpu.make_async_copy(rest, rest, send_sems.at[index]).wait()

    def row_transform(source, way):
        sign = jnp.where(lax.broadcasted_iota(jnp.int32, (height, 128), 1) < 64, way, -way)
        results = []
        for j in range(chunks):
            cosine = dot(cos_ref[...], source[j])
            sine = dot(sin_ref[...], source[j])
            results.append((cosine + pltpu.roll(sine, 64, 1) * sign) * row_factor)
        return results

    column_forward(inputs_ref, win_ref, spatial_out)
    pl.semaphore_wait(barrier, devices - 1)
    messages(spatial_out, spatial_in, 0)
    column_forward(strip_ref, wout_ref, grad_out)
    messages(grad_out, grad_in, 1)
    arrived(spatial_in, 0)
    freq = row_transform([spatial_in[j].reshape(height, 128) for j in range(chunks)], 1.0)
    pre_mix = dot(jnp.concatenate(freq, axis=1).astype(jnp.bfloat16), wmix_ref[...])
    gate = jax.nn.sigmoid(pre_mix)
    slope_ref[...] = gate * (1.0 + pre_mix * (1.0 - gate))
    arrived(grad_in, 1)
    freq = row_transform([grad_in[j].reshape(height, 128) for j in range(chunks)], 1.0)
    grad_mix = (jnp.concatenate(freq, axis=1) * slope_ref[...]).astype(jnp.bfloat16)
    mixed = dot(grad_mix, wmix_t_ref[...]).astype(jnp.bfloat16)
    back = row_transform([mixed[:, j * 128 : (j + 1) * 128] for j in range(chunks)], -1.0)
    for j in range(chunks):
        back_out[j] = back[j].astype(jnp.bfloat16).reshape(devices, 2, 128)
    messages(back_out, back_in, 2)
    arrived(back_in, 2)
    for j in range(chunks):
        block = back_in[j].reshape(2 * freqs, 128).astype(jnp.float32)
        both = jnp.concatenate([jnp.where(even_row, block, 0.0), jnp.where(even_row, 0.0, block)], axis=1)
        both = both.astype(jnp.bfloat16)
        cosine = dot(col_cos_t[...], both)
        sine = dot(col_sin_t[...], both)
        for i in range(2):
            piece = slice(i * 128, (i + 1) * 128)
            total = (cosine[:, piece] + pltpu.roll(sine[:, piece], 64, 1)) * col_factor
            keep = lax.broadcasted_iota(jnp.int32, (width, 128), 1) < 64
            out_ref[i, :, j * 128 : (j + 1) * 128] = jnp.where(keep, total, 0.0).astype(jnp.bfloat16)
    sent(spatial_out, 0)
    sent(grad_out, 1)
    sent(back_out, 2)


def spectral(inputs, strip_grad, weight_in, weight_out, weight_mix):
    rows, cols = lax.axis_size("row"), lax.axis_size("col")
    devices = rows * cols
    width = inputs.shape[1]
    height = inputs.shape[0] * devices
    chunks = weight_in.shape[1] // 64
    lanes = chunks * 128
    cos_table, sin_table = host_tables(width)
    mix = interleaved(weight_mix)
    exchange = pltpu.VMEM((chunks, devices, 2, 128), jnp.bfloat16)
    table = pltpu.VMEM((width, width), jnp.bfloat16)
    vmem = pl.BlockSpec(memory_space=pltpu.VMEM)
    return pl.pallas_call(
        functools.partial(spectral_kernel, (rows, cols, height, width, chunks)),
        out_shape=jax.ShapeDtypeStruct((2, width, lanes), jnp.bfloat16),
        in_specs=[vmem] * 8,
        out_specs=vmem,
        scratch_shapes=[exchange] * 6
        + [table] * 4
        + [
            pltpu.VMEM((2, width, lanes), jnp.bfloat16),
            pltpu.VMEM((height, lanes), jnp.float32),
            pltpu.SemaphoreType.DMA((3,)),
            pltpu.SemaphoreType.DMA((3,)),
        ],
        compiler_params=pltpu.CompilerParams(collective_id=0, has_side_effects=True, vmem_limit_bytes=48 * 2**20),
        name="spectral",
    )(
        inputs,
        strip_grad,
        duplicated(weight_in),
        duplicated(weight_out.T),
        mix,
        mix.T,
        jnp.asarray(cos_table),
        jnp.asarray(sin_table),
    )


def padded_out(weight_in):
    depth, width = weight_in.shape
    chunks = weight_in.T.reshape(width // 64, 64, depth)
    return jnp.concatenate([chunks, jnp.zeros_like(chunks)], axis=1).reshape(2 * width, depth)


def shards(
    features,
    target,
    hole_mask,
    kernel_first,
    kernel_second,
    inputs,
    weight_in,
    weight_out,
    weight_local,
    weight_mix,
):
    tile_rows = features.shape[0]
    tile_cols = features.shape[1]
    row_devices = lax.axis_size("row")
    col_devices = lax.axis_size("col")
    height = tile_rows * row_devices
    grid_width = tile_cols * col_devices
    wide_feat = padded_2(features, (("row", 0), ("col", 1)), 4)
    pre_wide = conv_valid(wide_feat, kernel_first)
    row_ids = lax.axis_index("row") * tile_rows - 2 + jnp.arange(tile_rows + 4, dtype=jnp.int32)
    col_ids = lax.axis_index("col") * tile_cols - 2 + jnp.arange(tile_cols + 4, dtype=jnp.int32)
    row_inside = (row_ids >= 0) & (row_ids < height)
    col_inside = (col_ids >= 0) & (col_ids < grid_width)
    inside_mask = row_inside[:, None] & col_inside[None, :]
    act_wide = jnp.where(inside_mask[:, :, None], jax.nn.silu(pre_wide), 0.0).astype(jnp.bfloat16)
    pre_first = pre_wide[2:-2, 2:-2]
    pre_second = conv_valid(act_wide, kernel_second)
    hole_weight = 1.0 + 2.0 * hole_mask.astype(jnp.float32)
    loss_grad = (hole_weight[:, :, None] * (pre_second - target.astype(jnp.float32))).astype(
        jnp.bfloat16
    )
    loss_wide = padded_2(loss_grad, (("row", 0), ("col", 1)), 2)
    grad_act = conv_valid(loss_wide, adjoint_kernel(kernel_second))
    grad_pre = (grad_act * silu_slope(pre_first)).astype(jnp.bfloat16)
    grad_wide = padded_2(grad_pre, (("row", 0), ("col", 1)), 2)
    grad_feat = conv_valid(grad_wide, adjoint_kernel(kernel_first)).astype(jnp.bfloat16)
    strip_grad = lax.all_to_all(grad_feat, "col", split_axis=0, concat_axis=1, tiled=True)
    spatial_grad = spectral(inputs, strip_grad, weight_in, weight_out, weight_mix)
    joined = jnp.concatenate([spatial_grad, strip_grad], axis=-1)
    weights = jnp.concatenate([padded_out(weight_in), weight_local.T], axis=0)
    return jnp.einsum("rwc,cf->rwf", joined, weights, preferred_element_type=jnp.float32).astype(jnp.bfloat16)


def solution(mesh):
    in_specs = (
        P("row", "col", None),
        P("row", "col", None),
        P("row", "col"),
        P(),
        P(),
        P(("row", "col"), None, None),
        P(),
        P(),
        P(),
        P(),
    )
    out_specs = P(("row", "col"), None, None)
    return jax.shard_map(shards, mesh=mesh, in_specs=in_specs, out_specs=out_specs, check_vma=False)
```

```python
import functools
import math

import jax
import jax.numpy as jnp
import numpy as np
from jax import lax
from jax.experimental import pallas as pl
from jax.experimental.pallas import tpu as pltpu
from jax.sharding import PartitionSpec as P

MESH = pl.DeviceIdType.MESH
SIDES = [(-1, 0), (1, 0), (-1, -1), (-1, 1), (1, -1), (1, 1), (0, -1), (0, 1)]


def host_tables(length):
    ids = np.arange(length, dtype=np.int64)
    angles = (2.0 * np.pi / length) * ((ids[:, None] * ids[None, :]) % length)
    return (np.cos(angles).astype(jnp.bfloat16), np.sin(angles).astype(jnp.bfloat16))


def dot(left, right):
    return jnp.dot(left, right, preferred_element_type=jnp.float32)


def dot_t(left, right):
    return lax.dot_general(left, right, (((1,), (1,)), ((), ())), preferred_element_type=jnp.float32)


def ids(shape, dim):
    return lax.broadcasted_iota(jnp.int32, shape, dim)


def ones_where(condition):
    return jnp.where(condition, 1.0, 0.0).astype(jnp.bfloat16)


def block_kernel(
    sizes,
    features_any,
    target_any,
    mask_any,
    first_any,
    second_any,
    inputs_any,
    win_any,
    wout_any,
    wlocal_any,
    wmix_any,
    cos_any,
    sin_any,
    joined_ref,
    weights_ref,
    target_ref,
    mask_ref,
    first_ref,
    second_ref,
    inputs_ref,
    win_ref,
    wout_ref,
    wlocal_ref,
    wmix_ref,
    cos_ref,
    sin_ref,
    feat_ext,
    act_ext,
    loss_ext,
    pre_ext,
    slope_first,
    hole_ref,
    first_adj,
    second_adj,
    grad_feat,
    strip_ref,
    spatial_out,
    spatial_in,
    grad_out,
    grad_in,
    back_out,
    back_in,
    col_cos,
    col_sin,
    col_cos_t,
    col_sin_t,
    held,
    slope_mix,
    win_double,
    wout_double,
    wmix_mixed,
    load_sems,
    halo_send,
    halo_recv,
    strip_send,
    strip_recv,
    send_sems,
    recv_sems,
):
    rows, cols, height, width, chunks, tile_rows, tile_cols, channels, edge = sizes
    devices = rows * cols
    half_width = chunks * 64
    lanes = chunks * 128
    freqs = width // 2
    col_factor = 1.0 / math.sqrt(width)
    row_factor = 1.0 / math.sqrt(height)
    my_row = lax.axis_index("row")
    my_col = lax.axis_index("col")
    me = my_row * cols + my_col
    barrier = pltpu.get_barrier_semaphore()

    def peer_of(step):
        return lax.rem(me + lax.rem(step * 77, devices), devices)

    def place(peer):
        return {"row": lax.div(peer, cols), "col": lax.rem(peer, cols)}

    def greet(step, carry):
        pl.semaphore_signal(barrier, inc=1, device_id=place(peer_of(step)), device_id_type=MESH)
        return carry

    lax.fori_loop(1, devices, greet, 0)

    center = (slice(4, 4 + tile_rows), slice(edge, edge + tile_cols))
    loads = [
        pltpu.make_async_copy(source, target, load_sems.at[index])
        for index, (source, target) in enumerate(
            [
                (win_any, win_ref),
                (inputs_any, inputs_ref),
                (cos_any, cos_ref),
                (sin_any, sin_ref),
                (first_any, first_ref),
                (second_any, second_ref),
                (features_any, feat_ext.at[pl.ds(4, tile_rows), pl.ds(edge, tile_cols)]),
                (wout_any, wout_ref),
                (wmix_any, wmix_ref),
                (mask_any, mask_ref),
                (target_any, target_ref),
                (wlocal_any, wlocal_ref),
            ]
        )
    ]
    for load in loads:
        load.start()

    def region(side, extent, thick, offset):
        if side < 0:
            return (offset, thick)
        if side > 0:
            return (offset + extent - thick, thick)
        return (offset, extent)

    def landing(side, extent, thick):
        if side < 0:
            return (extent + thick, thick)
        if side > 0:
            return (0, thick)
        return (thick, extent)

    def halo_copy(stage, side, source, target, thick, row_offset, col_offset):
        index = SIDES.index(side)
        source_rows = region(side[0], tile_rows, thick, row_offset)
        source_cols = region(side[1], tile_cols, edge, col_offset)
        target_rows = landing(side[0], tile_rows, thick)
        target_cols = landing(side[1], tile_cols, edge)
        return pltpu.make_async_remote_copy(
            src_ref=source.at[pl.ds(*source_rows), pl.ds(*source_cols)],
            dst_ref=target.at[pl.ds(*target_rows), pl.ds(*target_cols)],
            send_sem=halo_send.at[stage, index],
            recv_sem=halo_recv.at[stage, index],
            device_id={
                "row": lax.rem(my_row + side[0] + rows, rows),
                "col": lax.rem(my_col + side[1] + cols, cols),
            },
            device_id_type=MESH,
        )

    def clear_rows(ext, thick):
        @pl.when(my_row == 0)
        def _():
            ext[0:thick] = jnp.zeros_like(ext[0:thick])

        @pl.when(my_row == rows - 1)
        def _():
            ext[thick + tile_rows :] = jnp.zeros_like(ext[thick + tile_rows :])

    def clear_cols(ext):
        @pl.when(my_col == 0)
        def _():
            ext[:, 0:edge] = jnp.zeros_like(ext[:, 0:edge])

        @pl.when(my_col == cols - 1)
        def _():
            ext[:, edge + tile_cols :] = jnp.zeros_like(ext[:, edge + tile_cols :])

    def conv_rows(ext, pieces, first_col, count, kernel):
        taps = []
        for a in range(3):
            for b in range(3):
                parts = [
                    ext[start + 2 * a : start + 2 * a + n, first_col + 2 * b : first_col + 2 * b + count, :]
                    for start, n in pieces
                ]
                joint = parts[0] if len(parts) == 1 else jnp.concatenate(parts, axis=0)
                taps.append(joint.reshape(joint.shape[0] * count, channels))
        return dot(jnp.concatenate(taps, axis=1), kernel[...])

    even_row = ids((2 * freqs, 128), 0) % 2 == 0
    low_lane = ids((2 * freqs, 128), 1) < 64

    def column_forward(target):
        for j in range(chunks):
            piece = slice(j * 128, (j + 1) * 128)
            both = jnp.concatenate([held[0, :, piece], held[1, :, piece]], axis=1)
            cosine = dot(col_cos[...], both)
            sine = dot(col_sin[...], both)
            first = jnp.where(low_lane, cosine[:, :128], sine[:, :128])
            second = jnp.where(low_lane, cosine[:, 128:], sine[:, 128:])
            mixed_rows = (jnp.where(even_row, first, second) * col_factor).astype(jnp.bfloat16)
            target[j] = mixed_rows.reshape(freqs, 2, 128)

    def messages(source, target, index):
        def send(step, carry):
            peer = peer_of(step)
            pltpu.make_async_remote_copy(
                src_ref=source.at[:, peer],
                dst_ref=target.at[:, me],
                send_sem=send_sems.at[index],
                recv_sem=recv_sems.at[index],
                device_id=place(peer),
                device_id_type=MESH,
            ).start()
            return carry

        lax.fori_loop(1, devices, send, 0)
        pltpu.make_async_copy(source.at[:, me], target.at[:, me], recv_sems.at[index]).start()

    def arrived(target, index):
        pltpu.make_async_copy(target, target, recv_sems.at[index]).wait()

    def sent(source, index):
        rest = source.at[:, pl.ds(0, devices - 1)]
        pltpu.make_async_copy(rest, rest, send_sems.at[index]).wait()

    def row_transform(source, way):
        sign = jnp.where(ids((height, 128), 1) < 64, way, -way)
        results = []
        for j in range(chunks):
            cosine = dot(cos_ref[...], source[j])
            sine = dot(sin_ref[...], source[j])
            results.append((cosine + pltpu.roll(sine, 64, 1) * sign) * row_factor)
        return results

    pl.semaphore_wait(barrier, devices - 1)
    features_out = [halo_copy(0, side, features_any, feat_ext, 4, 0, 0) for side in SIDES]
    for copy in features_out:
        copy.start()

    loads[0].wait()
    double = ones_where(ids((half_width, lanes), 0) == 64 * (ids((half_width, lanes), 1) // 128) + ids((half_width, lanes), 1) % 64)
    win_double[...] = dot(win_ref[...], double).astype(jnp.bfloat16)
    loads[1].wait()
    for i in range(2):
        held[i] = dot(inputs_ref[i], win_double[...]).astype(jnp.bfloat16)
    loads[2].wait()
    loads[3].wait()
    pick = ones_where(ids((2 * freqs, freqs), 0) // 2 == ids((2 * freqs, freqs), 1))
    pick_t = ones_where(ids((freqs, 2 * freqs), 1) // 2 == ids((freqs, 2 * freqs), 0))
    alternate = (1 - 2 * (ids((2 * freqs, width), 1) % 2)).astype(jnp.float32)
    alternate_t = (1 - 2 * (ids((width, 2 * freqs), 0) % 2)).astype(jnp.float32)
    col_cos[...] = dot(pick, cos_ref[:freqs, :]).astype(jnp.bfloat16)
    col_sin[...] = jnp.where(ids((2 * freqs, width), 0) < 2, alternate, -dot(pick, sin_ref[:freqs, :])).astype(jnp.bfloat16)
    column_forward(spatial_out)
    messages(spatial_out, spatial_in, 0)
    loads[4].wait()
    for index in (6, 7):
        features_out[index].wait_recv()
    loads[6].wait()
    clear_cols(feat_ext.at[pl.ds(4, tile_rows)])

    wide = tile_cols + edge
    margin = edge // 2

    def first_conv(start):
        pre = conv_rows(feat_ext, [(start, 4)], edge - margin - 2, wide, first_ref)
        gate = jax.nn.sigmoid(pre)
        act = (pre * gate).reshape(4, wide, channels)
        row_id = my_row * tile_rows - 2 + start + ids((4, wide, channels), 0)
        col_id = my_col * tile_cols - margin + ids((4, wide, channels), 1)
        inside = (row_id >= 0) & (row_id < height) & (col_id >= 0) & (col_id < width)
        act_ext[start : start + 4, edge - margin : edge - margin + wide, :] = jnp.where(inside, act, 0.0).astype(jnp.bfloat16)
        slope = (gate * (1.0 + pre * (1.0 - gate))).reshape(4, wide, channels)
        low, high = max(start, 2), min(start + 4, 2 + tile_rows)
        slope_first[low - 2 : high - 2] = slope[low - start : high - start, margin : margin + tile_cols, :]

    first_conv(4)

    loads[5].wait()
    eye = ones_where(ids((channels, channels), 0) == ids((channels, channels), 1))
    for source, target in ((first_ref, first_adj), (second_ref, second_adj)):
        for tap in range(9):
            block = source[(8 - tap) * channels : (9 - tap) * channels, :]
            target[tap * channels : (tap + 1) * channels, :] = dot_t(eye, block).astype(jnp.bfloat16)
    loads[9].wait()
    spot = ids((tile_cols, tile_cols), 0) == ids((tile_cols, tile_cols), 1)
    for p in range(tile_rows):
        line = mask_ref[p : p + 1, :].astype(jnp.float32)
        spread = jnp.where(spot, line, 0.0).astype(jnp.bfloat16)
        hole_ref[p] = 1.0 + 2.0 * dot(spread, jnp.ones((tile_cols, channels), jnp.bfloat16))
    for copy in features_out[:6]:
        copy.wait_recv()
    clear_rows(feat_ext, 4)
    clear_cols(feat_ext)
    first_conv(0)
    first_conv(8)

    outer = [(0, 2), (tile_rows - 2, 2)]
    inner = [(2, tile_rows - 4)]

    def store(ext, pieces, value, thick):
        at = 0
        for start, n in pieces:
            ext[start + thick : start + thick + n, edge : edge + tile_cols, :] = value[at : at + n]
            at += n

    def gather(ref, pieces):
        parts = [ref[start : start + n] for start, n in pieces]
        return parts[0] if len(parts) == 1 else jnp.concatenate(parts, axis=0)

    def second_conv(pieces):
        pre = conv_rows(act_ext, pieces, edge - 2, tile_cols, second_ref)
        pre = pre.reshape(pre.shape[0] // tile_cols, tile_cols, channels)
        loss = gather(hole_ref, pieces) * (pre - gather(target_ref, pieces).astype(jnp.float32))
        store(loss_ext, pieces, loss.astype(jnp.bfloat16), 2)

    loads[10].wait()
    loss_out = [halo_copy(1, side, loss_ext, loss_ext, 2, 2, edge) for side in SIDES]
    second_conv(outer)
    for copy in loss_out[:6]:
        copy.start()
    second_conv(inner)
    for copy in loss_out[6:]:
        copy.start()
    for copy in loss_out[6:]:
        copy.wait_recv()
    clear_cols(loss_ext.at[pl.ds(2, tile_rows)])

    def third_conv(pieces):
        value = conv_rows(loss_ext, pieces, edge - 2, tile_cols, second_adj)
        value = value.reshape(value.shape[0] // tile_cols, tile_cols, channels) * gather(slope_first, pieces)
        store(pre_ext, pieces, value.astype(jnp.bfloat16), 2)

    third_conv(inner)
    for copy in loss_out[:6]:
        copy.wait_recv()
    clear_rows(loss_ext, 2)
    clear_cols(loss_ext)
    pre_out = [halo_copy(2, side, pre_ext, pre_ext, 2, 2, edge) for side in SIDES]
    third_conv(outer)
    for copy in pre_out:
        copy.start()

    col_cos_t[...] = dot(cos_ref[:, :freqs], pick_t).astype(jnp.bfloat16)
    col_sin_t[...] = jnp.where(ids((width, 2 * freqs), 1) < 2, alternate_t, -dot(sin_ref[:, :freqs], pick_t)).astype(jnp.bfloat16)
    loads[7].wait()
    double_t = ones_where(ids((lanes, half_width), 1) == 64 * (ids((lanes, half_width), 0) // 128) + ids((lanes, half_width), 0) % 64)
    wout_double[...] = dot(double_t, wout_ref[...]).astype(jnp.bfloat16)

    def place_of(lane):
        return ((lane % 128) // 64) * half_width + 64 * (lane // 128) + lane % 64

    order = ones_where(ids((lanes, lanes), 0) == place_of(ids((lanes, lanes), 1)))
    order_t = ones_where(ids((lanes, lanes), 1) == place_of(ids((lanes, lanes), 0)))
    loads[8].wait()
    partly = dot(order_t, wmix_ref[...]).astype(jnp.bfloat16)
    wmix_mixed[...] = dot(partly, order).astype(jnp.bfloat16)
    loads[11].wait()
    low_half = ids((win_double.shape[0], lanes), 1) % 128 < 64
    weights_ref[:, :lanes] = jnp.where(low_half, win_double[...].astype(jnp.float32), 0.0).astype(jnp.bfloat16)
    weights_ref[:, lanes:] = wlocal_ref[...]

    for copy in pre_out[6:]:
        copy.wait_recv()
    clear_cols(pre_ext.at[pl.ds(2, tile_rows)])

    def fourth_conv(pieces):
        value = conv_rows(pre_ext, pieces, edge - 2, tile_cols, first_adj).astype(jnp.bfloat16)
        value = value.reshape(value.shape[0] // tile_cols, tile_cols, channels)
        at = 0
        for start, n in pieces:
            grad_feat[start : start + n] = value[at : at + n]
            at += n

    def strip_send_to(hop):
        peer_col = lax.rem(my_col + hop, cols)
        return pltpu.make_async_remote_copy(
            src_ref=grad_feat.at[pl.ds(2 * peer_col, 2)],
            dst_ref=strip_ref.at[:, pl.ds(pl.multiple_of(my_col * tile_cols, tile_cols), tile_cols)],
            send_sem=strip_send.at[hop],
            recv_sem=strip_recv.at[hop],
            device_id={"row": my_row, "col": peer_col},
            device_id_type=MESH,
        )

    fourth_conv(inner)
    for copy in pre_out[:6]:
        copy.wait_recv()
    clear_rows(pre_ext, 2)
    clear_cols(pre_ext)
    fourth_conv(outer)
    strips_out = [strip_send_to(hop) for hop in range(1, cols)]
    for copy in strips_out:
        copy.start()
    own_strip = pltpu.make_async_copy(
        grad_feat.at[pl.ds(2 * my_col, 2)],
        strip_ref.at[:, pl.ds(pl.multiple_of(my_col * tile_cols, tile_cols), tile_cols)],
        strip_recv.at[0],
    )
    own_strip.start()

    arrived(spatial_in, 0)
    freq = row_transform([spatial_in[j].reshape(height, 128) for j in range(chunks)], 1.0)
    pre_mix = dot(jnp.concatenate(freq, axis=1).astype(jnp.bfloat16), wmix_mixed[...])
    gate = jax.nn.sigmoid(pre_mix)
    slope_mix[...] = gate * (1.0 + pre_mix * (1.0 - gate))

    own_strip.wait()
    for copy in strips_out:
        copy.wait_recv()
    for i in range(2):
        held[i] = dot_t(strip_ref[i], wout_double[...]).astype(jnp.bfloat16)
    column_forward(grad_out)
    messages(grad_out, grad_in, 1)
    joined_ref[:, :, lanes:] = strip_ref[...]
    arrived(grad_in, 1)
    freq = row_transform([grad_in[j].reshape(height, 128) for j in range(chunks)], 1.0)
    grad_mix = (jnp.concatenate(freq, axis=1) * slope_mix[...]).astype(jnp.bfloat16)
    mixed = dot_t(grad_mix, wmix_mixed[...]).astype(jnp.bfloat16)
    back = row_transform([mixed[:, j * 128 : (j + 1) * 128] for j in range(chunks)], -1.0)
    for j in range(chunks):
        back_out[j] = back[j].astype(jnp.bfloat16).reshape(devices, 2, 128)
    messages(back_out, back_in, 2)
    for copy in features_out + loss_out + pre_out + strips_out:
        copy.wait_send()
    sent(spatial_out, 0)
    sent(grad_out, 1)
    arrived(back_in, 2)
    keep = ids((width, 128), 1) < 64
    for j in range(chunks):
        block = back_in[j].reshape(2 * freqs, 128).astype(jnp.float32)
        both = jnp.concatenate([jnp.where(even_row, block, 0.0), jnp.where(even_row, 0.0, block)], axis=1)
        both = both.astype(jnp.bfloat16)
        cosine = dot(col_cos_t[...], both)
        sine = dot(col_sin_t[...], both)
        for i in range(2):
            piece = slice(i * 128, (i + 1) * 128)
            total = (cosine[:, piece] + pltpu.roll(sine[:, piece], 64, 1)) * col_factor
            joined_ref[i, :, j * 128 : (j + 1) * 128] = jnp.where(keep, total, 0.0).astype(jnp.bfloat16)
    sent(back_out, 2)


def shards(
    features,
    target,
    hole_mask,
    kernel_first,
    kernel_second,
    inputs,
    weight_in,
    weight_out,
    weight_local,
    weight_mix,
):
    rows, cols = lax.axis_size("row"), lax.axis_size("col")
    devices = rows * cols
    tile_rows, tile_cols, channels = features.shape
    width = inputs.shape[1]
    height = inputs.shape[0] * devices
    depth = inputs.shape[2]
    chunks = weight_in.shape[1] // 64
    lanes = chunks * 128
    edge = min(16, tile_cols)
    cos_table, sin_table = host_tables(width)
    wide = tile_cols + 2 * edge
    bf16, f32 = jnp.bfloat16, jnp.float32
    operands = (
        features,
        target,
        hole_mask,
        kernel_first.reshape(9 * channels, channels),
        kernel_second.reshape(9 * channels, channels),
        inputs,
        weight_in,
        weight_out,
        weight_local,
        weight_mix,
        jnp.asarray(cos_table),
        jnp.asarray(sin_table),
    )
    exchange = pltpu.VMEM((chunks, devices, 2, 128), bf16)
    table = pltpu.VMEM((width, width), bf16)
    kernel_shape = pltpu.VMEM((9 * channels, channels), bf16)
    vmem = pl.BlockSpec(memory_space=pltpu.VMEM)
    joined, weights = pl.pallas_call(
        functools.partial(
            block_kernel, (rows, cols, height, width, chunks, tile_rows, tile_cols, channels, edge)
        ),
        out_shape=(
            jax.ShapeDtypeStruct((2, width, lanes + channels), bf16),
            jax.ShapeDtypeStruct((depth, lanes + channels), bf16),
        ),
        in_specs=[pl.BlockSpec(memory_space=pl.ANY)] * len(operands),
        out_specs=(vmem, vmem),
        scratch_shapes=[pltpu.VMEM(item.shape, item.dtype) for item in operands[1:]]
        + [
            pltpu.VMEM((tile_rows + 8, wide, channels), bf16),
            pltpu.VMEM((tile_rows + 4, wide, channels), bf16),
            pltpu.VMEM((tile_rows + 4, wide, channels), bf16),
            pltpu.VMEM((tile_rows + 4, wide, channels), bf16),
            pltpu.VMEM((tile_rows, tile_cols, channels), f32),
            pltpu.VMEM((tile_rows, tile_cols, channels), f32),
            kernel_shape,
            kernel_shape,
            pltpu.VMEM((tile_rows, tile_cols, channels), bf16),
            pltpu.VMEM((2, width, channels), bf16),
        ]
        + [exchange] * 6
        + [table] * 4
        + [
            pltpu.VMEM((2, width, lanes), bf16),
            pltpu.VMEM((height, lanes), f32),
            pltpu.VMEM((depth, lanes), bf16),
            pltpu.VMEM((lanes, channels), bf16),
            pltpu.VMEM((lanes, lanes), bf16),
            pltpu.SemaphoreType.DMA((len(operands),)),
            pltpu.SemaphoreType.DMA((3, 8)),
            pltpu.SemaphoreType.DMA((3, 8)),
            pltpu.SemaphoreType.DMA((cols,)),
            pltpu.SemaphoreType.DMA((cols,)),
            pltpu.SemaphoreType.DMA((3,)),
            pltpu.SemaphoreType.DMA((3,)),
        ],
        compiler_params=pltpu.CompilerParams(
            collective_id=0, has_side_effects=True, vmem_limit_bytes=56 * 2**20
        ),
        name="block",
    )(*operands)
    total = jnp.einsum("rwc,fc->rwf", joined, weights, preferred_element_type=f32)
    return total.astype(bf16)


def solution(mesh):
    in_specs = (
        P("row", "col", None),
        P("row", "col", None),
        P("row", "col"),
        P(),
        P(),
        P(("row", "col"), None, None),
        P(),
        P(),
        P(),
        P(),
    )
    out_specs = P(("row", "col"), None, None)
    return jax.shard_map(shards, mesh=mesh, in_specs=in_specs, out_specs=out_specs, check_vma=False)
```

```python
import functools
import math

import jax
import jax.numpy as jnp
import numpy as np
from jax import lax
from jax.experimental import pallas as pl
from jax.experimental.pallas import tpu as pltpu
from jax.sharding import PartitionSpec as P

MESH = pl.DeviceIdType.MESH
SIDES = [(0, -1), (0, 1), (-1, 0), (1, 0), (-1, -1), (-1, 1), (1, -1), (1, 1)]
UNROLL = 8


def host_tables(length):
    ids = np.arange(length, dtype=np.int64)
    angles = (2.0 * np.pi / length) * ((ids[:, None] * ids[None, :]) % length)
    return (np.cos(angles).astype(jnp.bfloat16), np.sin(angles).astype(jnp.bfloat16))


def dot(left, right):
    return jnp.dot(left, right, preferred_element_type=jnp.float32)


def dot_t(left, right):
    return lax.dot_general(left, right, (((1,), (1,)), ((), ())), preferred_element_type=jnp.float32)


def ids(shape, dim):
    return lax.broadcasted_iota(jnp.int32, shape, dim)


def ones_where(condition):
    return jnp.where(condition, 1.0, 0.0).astype(jnp.bfloat16)


def block_kernel(
    sizes,
    features_any,
    target_any,
    mask_any,
    first_any,
    second_any,
    inputs_any,
    win_any,
    wout_any,
    wlocal_any,
    wmix_any,
    cos_any,
    sin_any,
    joined_ref,
    weights_ref,
    target_ref,
    mask_ref,
    first_ref,
    second_ref,
    inputs_ref,
    win_ref,
    wout_ref,
    wlocal_ref,
    wmix_ref,
    cos_ref,
    sin_ref,
    feat_ext,
    act_ext,
    loss_ext,
    pre_ext,
    slope_first,
    hole_ref,
    first_adj,
    second_adj,
    grad_feat,
    strip_ref,
    spatial_out,
    spatial_in,
    grad_out,
    grad_in,
    back_out,
    back_in,
    col_cos,
    col_sin,
    col_cos_t,
    col_sin_t,
    held,
    slope_mix,
    win_double,
    wout_double,
    wmix_mixed,
    load_sems,
    halo_send,
    halo_recv,
    strip_send,
    strip_recv,
    send_sems,
    recv_sems,
):
    rows, cols, height, width, chunks, tile_rows, tile_cols, channels, edge = sizes
    devices = rows * cols
    half_width = chunks * 64
    lanes = chunks * 128
    freqs = width // 2
    col_factor = 1.0 / math.sqrt(width)
    row_factor = 1.0 / math.sqrt(height)
    my_row = lax.axis_index("row")
    my_col = lax.axis_index("col")
    me = my_row * cols + my_col
    barrier = pltpu.get_barrier_semaphore()

    def each_peer(action, low=0, high=cols):
        for hop in range(low, high):
            col = lax.rem(my_col + hop, cols)
            per_turn = math.gcd(UNROLL, rows)

            def turn(index, carry, hop=hop, col=col):
                for k in range(per_turn):
                    action(lax.rem(my_row + (index * per_turn + k) * 21, rows), col)
                return carry

            if hop == 0:
                for k in range(1, per_turn):
                    action(lax.rem(my_row + k * 21, rows), col)
            lax.fori_loop(1 if hop == 0 else 0, rows // per_turn, turn, 0)

    def greet(row, col):
        pl.semaphore_signal(barrier, inc=1, device_id={"row": row, "col": col}, device_id_type=MESH)

    each_peer(greet)

    loads = [
        pltpu.make_async_copy(source, target, load_sems.at[index])
        for index, (source, target) in enumerate(
            [
                (win_any, win_ref),
                (inputs_any, inputs_ref),
                (cos_any, cos_ref),
                (sin_any, sin_ref),
                (first_any, first_ref),
                (second_any, second_ref),
                (features_any, feat_ext.at[pl.ds(4, tile_rows), pl.ds(edge, tile_cols)]),
                (wout_any, wout_ref),
                (wmix_any, wmix_ref),
                (mask_any, mask_ref),
                (target_any, target_ref),
                (wlocal_any, wlocal_ref),
            ]
        )
    ]
    for load in loads:
        load.start()

    def region(side, extent, thick, offset):
        if side < 0:
            return (offset, thick)
        if side > 0:
            return (offset + extent - thick, thick)
        return (offset, extent)

    def landing(side, extent, thick):
        if side < 0:
            return (extent + thick, thick)
        if side > 0:
            return (0, thick)
        return (thick, extent)

    def halo_copy(stage, side, source, target, thick, row_offset, col_offset):
        index = SIDES.index(side)
        source_rows = region(side[0], tile_rows, thick, row_offset)
        source_cols = region(side[1], tile_cols, edge, col_offset)
        target_rows = landing(side[0], tile_rows, thick)
        target_cols = landing(side[1], tile_cols, edge)
        return pltpu.make_async_remote_copy(
            src_ref=source.at[pl.ds(*source_rows), pl.ds(*source_cols)],
            dst_ref=target.at[pl.ds(*target_rows), pl.ds(*target_cols)],
            send_sem=halo_send.at[stage, index],
            recv_sem=halo_recv.at[stage, index],
            device_id={
                "row": lax.rem(my_row + side[0] + rows, rows),
                "col": lax.rem(my_col + side[1] + cols, cols),
            },
            device_id_type=MESH,
        )

    def exists(side, way):
        row, col = my_row + way * side[0], my_col + way * side[1]
        return (row >= 0) & (row < rows) & (col >= 0) & (col < cols)

    def begin(copies, indices):
        for index in indices:
            pl.when(exists(SIDES[index], 1))(copies[index].start)

    def receive(copies, indices):
        for index in indices:
            pl.when(exists(SIDES[index], -1))(copies[index].wait_recv)

    def flush(copies):
        for index in range(8):
            pl.when(exists(SIDES[index], 1))(copies[index].wait_send)

    def clear_rows(ext, thick):
        @pl.when(my_row == 0)
        def _():
            ext[0:thick] = jnp.zeros_like(ext[0:thick])

        @pl.when(my_row == rows - 1)
        def _():
            ext[thick + tile_rows :] = jnp.zeros_like(ext[thick + tile_rows :])

    def clear_cols(ext):
        @pl.when(my_col == 0)
        def _():
            ext[:, 0:edge] = jnp.zeros_like(ext[:, 0:edge])

        @pl.when(my_col == cols - 1)
        def _():
            ext[:, edge + tile_cols :] = jnp.zeros_like(ext[:, edge + tile_cols :])

    def conv_rows(ext, pieces, first_col, count, kernel):
        taps = []
        for a in range(3):
            for b in range(3):
                parts = [
                    ext[start + 2 * a : start + 2 * a + n, first_col + 2 * b : first_col + 2 * b + count, :]
                    for start, n in pieces
                ]
                joint = parts[0] if len(parts) == 1 else jnp.concatenate(parts, axis=0)
                taps.append(joint.reshape(joint.shape[0] * count, channels))
        return dot(jnp.concatenate(taps, axis=1), kernel[...])

    for ext, thick in ((feat_ext, 4), (loss_ext, 2), (pre_ext, 2)):
        clear_rows(ext, thick)
        clear_cols(ext)

    even_row = ids((2 * freqs, 128), 0) % 2 == 0
    low_lane = ids((2 * freqs, 128), 1) < 64

    def column_forward(target):
        for j in range(chunks):
            piece = slice(j * 128, (j + 1) * 128)
            both = jnp.concatenate([held[0, :, piece], held[1, :, piece]], axis=1)
            cosine = dot(col_cos[...], both)
            sine = dot(col_sin[...], both)
            first = jnp.where(low_lane, cosine[:, :128], sine[:, :128])
            second = jnp.where(low_lane, cosine[:, 128:], sine[:, 128:])
            mixed_rows = (jnp.where(even_row, first, second) * col_factor).astype(jnp.bfloat16)
            target[j] = mixed_rows.reshape(freqs, 2, 128)

    def messages(source, target, index, low=0, high=cols):
        def send(row, col):
            pltpu.make_async_remote_copy(
                src_ref=source.at[:, row * cols + col],
                dst_ref=target.at[:, me],
                send_sem=send_sems.at[index],
                recv_sem=recv_sems.at[index],
                device_id={"row": row, "col": col},
                device_id_type=MESH,
            ).start()

        each_peer(send, low, high)
        if low == 0:
            pltpu.make_async_copy(source.at[:, me], target.at[:, me], recv_sems.at[index]).start()

    def arrived(target, index):
        pltpu.make_async_copy(target, target, recv_sems.at[index]).wait()

    def sent(source, index):
        rest = source.at[:, pl.ds(0, devices - 1)]
        pltpu.make_async_copy(rest, rest, send_sems.at[index]).wait()

    def row_transform(source, way):
        sign = jnp.where(ids((height, 128), 1) < 64, way, -way)
        results = []
        for j in range(chunks):
            cosine = dot(cos_ref[...], source[j])
            sine = dot(sin_ref[...], source[j])
            results.append((cosine + pltpu.roll(sine, 64, 1) * sign) * row_factor)
        return results

    pl.semaphore_wait(barrier, devices - 1)
    features_out = [halo_copy(0, side, features_any, feat_ext, 4, 0, 0) for side in SIDES]
    begin(features_out, range(8))

    loads[0].wait()
    double_t = ones_where(ids((lanes, half_width), 1) == 64 * (ids((lanes, half_width), 0) // 128) + ids((lanes, half_width), 0) % 64)
    win_double[...] = dot(double_t, win_ref[...]).astype(jnp.bfloat16)
    loads[1].wait()
    for i in range(2):
        held[i] = dot_t(inputs_ref[i], win_double[...]).astype(jnp.bfloat16)
    loads[2].wait()
    loads[3].wait()
    pick = ones_where(ids((2 * freqs, freqs), 0) // 2 == ids((2 * freqs, freqs), 1))
    pick_t = ones_where(ids((freqs, 2 * freqs), 1) // 2 == ids((freqs, 2 * freqs), 0))
    alternate = (1 - 2 * (ids((2 * freqs, width), 1) % 2)).astype(jnp.float32)
    alternate_t = (1 - 2 * (ids((width, 2 * freqs), 0) % 2)).astype(jnp.float32)
    col_cos[...] = dot(pick, cos_ref[:freqs, :]).astype(jnp.bfloat16)
    col_sin[...] = jnp.where(ids((2 * freqs, width), 0) < 2, alternate, -dot(pick, sin_ref[:freqs, :])).astype(jnp.bfloat16)
    column_forward(spatial_out)
    loads[4].wait()
    receive(features_out, (0, 1))
    loads[6].wait()

    wide = tile_cols + edge
    margin = edge // 2

    def first_conv(start):
        pre = conv_rows(feat_ext, [(start, 4)], edge - margin - 2, wide, first_ref)
        gate = jax.nn.sigmoid(pre)
        act = (pre * gate).reshape(4, wide, channels)
        row_id = my_row * tile_rows - 2 + start + ids((4, wide, channels), 0)
        col_id = my_col * tile_cols - margin + ids((4, wide, channels), 1)
        inside = (row_id >= 0) & (row_id < height) & (col_id >= 0) & (col_id < width)
        act_ext[start : start + 4, edge - margin : edge - margin + wide, :] = jnp.where(inside, act, 0.0).astype(jnp.bfloat16)
        slope = (gate * (1.0 + pre * (1.0 - gate))).reshape(4, wide, channels)
        low, high = max(start, 2), min(start + 4, 2 + tile_rows)
        slope_first[low - 2 : high - 2] = slope[low - start : high - start, margin : margin + tile_cols, :]

    first_conv(4)

    loads[5].wait()
    eye = ones_where(ids((channels, channels), 0) == ids((channels, channels), 1))
    for source, target in ((first_ref, first_adj), (second_ref, second_adj)):
        for tap in range(9):
            block = source[(8 - tap) * channels : (9 - tap) * channels, :]
            target[tap * channels : (tap + 1) * channels, :] = dot_t(eye, block).astype(jnp.bfloat16)
    loads[9].wait()
    spot = ids((tile_cols, tile_cols), 0) == ids((tile_cols, tile_cols), 1)
    for p in range(tile_rows):
        line = mask_ref[p : p + 1, :].astype(jnp.float32)
        spread = jnp.where(spot, line, 0.0).astype(jnp.bfloat16)
        hole_ref[p] = 1.0 + 2.0 * dot(spread, jnp.ones((tile_cols, channels), jnp.bfloat16))
    receive(features_out, range(2, 8))
    messages(spatial_out, spatial_in, 0, 0, 1)
    first_conv(0)
    first_conv(8)

    outer = [(0, 2), (tile_rows - 2, 2)]
    inner = [(2, tile_rows - 4)]

    def store(ext, pieces, value, thick):
        at = 0
        for start, n in pieces:
            ext[start + thick : start + thick + n, edge : edge + tile_cols, :] = value[at : at + n]
            at += n

    def gather(ref, pieces):
        parts = [ref[start : start + n] for start, n in pieces]
        return parts[0] if len(parts) == 1 else jnp.concatenate(parts, axis=0)

    def second_conv(pieces):
        pre = conv_rows(act_ext, pieces, edge - 2, tile_cols, second_ref)
        pre = pre.reshape(pre.shape[0] // tile_cols, tile_cols, channels)
        loss = gather(hole_ref, pieces) * (pre - gather(target_ref, pieces).astype(jnp.float32))
        store(loss_ext, pieces, loss.astype(jnp.bfloat16), 2)

    loads[10].wait()
    loss_out = [halo_copy(1, side, loss_ext, loss_ext, 2, 2, edge) for side in SIDES]
    second_conv(outer)
    begin(loss_out, range(2, 8))
    second_conv(inner)
    begin(loss_out, (0, 1))
    receive(loss_out, (0, 1))

    def third_conv(pieces):
        value = conv_rows(loss_ext, pieces, edge - 2, tile_cols, second_adj)
        value = value.reshape(value.shape[0] // tile_cols, tile_cols, channels) * gather(slope_first, pieces)
        store(pre_ext, pieces, value.astype(jnp.bfloat16), 2)

    third_conv(inner)
    receive(loss_out, range(2, 8))
    messages(spatial_out, spatial_in, 0, 1, 2)
    pre_out = [halo_copy(2, side, pre_ext, pre_ext, 2, 2, edge) for side in SIDES]
    third_conv(outer)
    begin(pre_out, range(8))

    col_cos_t[...] = dot(cos_ref[:, :freqs], pick_t).astype(jnp.bfloat16)
    col_sin_t[...] = jnp.where(ids((width, 2 * freqs), 1) < 2, alternate_t, -dot(sin_ref[:, :freqs], pick_t)).astype(jnp.bfloat16)
    loads[7].wait()
    wout_double[...] = dot(double_t, wout_ref[...]).astype(jnp.bfloat16)

    def place_of(lane):
        return ((lane % 128) // 64) * half_width + 64 * (lane // 128) + lane % 64

    order = ones_where(ids((lanes, lanes), 0) == place_of(ids((lanes, lanes), 1)))
    order_t = ones_where(ids((lanes, lanes), 1) == place_of(ids((lanes, lanes), 0)))
    loads[8].wait()
    partly = dot(order_t, wmix_ref[...]).astype(jnp.bfloat16)
    wmix_mixed[...] = dot(partly, order).astype(jnp.bfloat16)
    loads[11].wait()
    low_half = ids(win_double.shape, 0) % 128 < 64
    weights_ref[:lanes, :] = jnp.where(low_half, win_double[...].astype(jnp.float32), 0.0).astype(jnp.bfloat16)
    weights_ref[lanes:, :] = dot_t(eye, wlocal_ref[...]).astype(jnp.bfloat16)
    receive(pre_out, (0, 1))

    def fourth_conv(pieces):
        value = conv_rows(pre_ext, pieces, edge - 2, tile_cols, first_adj).astype(jnp.bfloat16)
        value = value.reshape(value.shape[0] // tile_cols, tile_cols, channels)
        at = 0
        for start, n in pieces:
            grad_feat[start : start + n] = value[at : at + n]
            at += n

    here = pl.ds(pl.multiple_of(my_col * tile_cols, tile_cols), tile_cols)

    def strip_copy(peer_col):
        return pltpu.make_async_remote_copy(
            src_ref=grad_feat.at[pl.ds(2 * peer_col, 2)],
            dst_ref=strip_ref.at[:, here],
            send_sem=strip_send.at[peer_col],
            recv_sem=strip_recv.at[my_col],
            device_id={"row": my_row, "col": peer_col},
            device_id_type=MESH,
        )

    def strip_own():
        return pltpu.make_async_copy(
            grad_feat.at[pl.ds(2 * my_col, 2)], strip_ref.at[:, here], strip_recv.at[my_col]
        )

    def strip_begin(peer_cols):
        for peer_col in peer_cols:
            pl.when(my_col != peer_col)(strip_copy(peer_col).start)
            pl.when(my_col == peer_col)(strip_own().start)

    def strip_receive():
        for peer_col in range(cols):
            part = strip_ref.at[:, pl.ds(peer_col * tile_cols, tile_cols)]
            pltpu.make_async_copy(part, part, strip_recv.at[peer_col]).wait()

    fourth_conv(inner)
    strip_begin(range(1, cols - 1))
    receive(pre_out, range(2, 8))
    messages(spatial_out, spatial_in, 0, 2, cols)
    fourth_conv(outer)
    strip_begin((0, cols - 1))

    strip_receive()
    for i in range(2):
        held[i] = dot_t(strip_ref[i], wout_double[...]).astype(jnp.bfloat16)
    column_forward(grad_out)
    messages(grad_out, grad_in, 1)
    joined_ref[:, :, lanes:] = strip_ref[...]

    arrived(spatial_in, 0)
    freq = row_transform([spatial_in[j].reshape(height, 128) for j in range(chunks)], 1.0)
    pre_mix = dot(jnp.concatenate(freq, axis=1).astype(jnp.bfloat16), wmix_mixed[...])
    gate = jax.nn.sigmoid(pre_mix)
    slope_mix[...] = gate * (1.0 + pre_mix * (1.0 - gate))

    arrived(grad_in, 1)
    freq = row_transform([grad_in[j].reshape(height, 128) for j in range(chunks)], 1.0)
    grad_mix = (jnp.concatenate(freq, axis=1) * slope_mix[...]).astype(jnp.bfloat16)
    mixed = dot_t(grad_mix, wmix_mixed[...]).astype(jnp.bfloat16)
    back = row_transform([mixed[:, j * 128 : (j + 1) * 128] for j in range(chunks)], -1.0)
    for j in range(chunks):
        back_out[j] = back[j].astype(jnp.bfloat16).reshape(devices, 2, 128)
    messages(back_out, back_in, 2)
    for copies in (features_out, loss_out, pre_out):
        flush(copies)
    for peer_col in range(cols):
        pl.when(my_col != peer_col)(strip_copy(peer_col).wait_send)
    sent(spatial_out, 0)
    sent(grad_out, 1)
    arrived(back_in, 2)
    keep = ids((width, 128), 1) < 64
    for j in range(chunks):
        block = back_in[j].reshape(2 * freqs, 128).astype(jnp.float32)
        both = jnp.concatenate([jnp.where(even_row, block, 0.0), jnp.where(even_row, 0.0, block)], axis=1)
        both = both.astype(jnp.bfloat16)
        cosine = dot(col_cos_t[...], both)
        sine = dot(col_sin_t[...], both)
        for i in range(2):
            piece = slice(i * 128, (i + 1) * 128)
            total = (cosine[:, piece] + pltpu.roll(sine[:, piece], 64, 1)) * col_factor
            joined_ref[i, :, j * 128 : (j + 1) * 128] = jnp.where(keep, total, 0.0).astype(jnp.bfloat16)
    sent(back_out, 2)


def shards(
    features,
    target,
    hole_mask,
    kernel_first,
    kernel_second,
    inputs,
    weight_in,
    weight_out,
    weight_local,
    weight_mix,
):
    rows, cols = lax.axis_size("row"), lax.axis_size("col")
    devices = rows * cols
    tile_rows, tile_cols, channels = features.shape
    width = inputs.shape[1]
    height = inputs.shape[0] * devices
    depth = inputs.shape[2]
    chunks = weight_in.shape[1] // 64
    lanes = chunks * 128
    edge = min(16, tile_cols)
    cos_table, sin_table = host_tables(width)
    wide = tile_cols + 2 * edge
    bf16, f32 = jnp.bfloat16, jnp.float32
    operands = (
        features,
        target,
        hole_mask,
        kernel_first.reshape(9 * channels, channels),
        kernel_second.reshape(9 * channels, channels),
        inputs,
        weight_in.T,
        weight_out,
        weight_local,
        weight_mix,
        jnp.asarray(cos_table),
        jnp.asarray(sin_table),
    )
    exchange = pltpu.VMEM((chunks, devices, 2, 128), bf16)
    table = pltpu.VMEM((width, width), bf16)
    kernel_shape = pltpu.VMEM((9 * channels, channels), bf16)
    vmem = pl.BlockSpec(memory_space=pltpu.VMEM)
    joined, weights = pl.pallas_call(
        functools.partial(
            block_kernel, (rows, cols, height, width, chunks, tile_rows, tile_cols, channels, edge)
        ),
        out_shape=(
            jax.ShapeDtypeStruct((2, width, lanes + channels), bf16),
            jax.ShapeDtypeStruct((lanes + channels, depth), bf16),
        ),
        in_specs=[pl.BlockSpec(memory_space=pl.ANY)] * len(operands),
        out_specs=(vmem, vmem),
        scratch_shapes=[pltpu.VMEM(item.shape, item.dtype) for item in operands[1:]]
        + [
            pltpu.VMEM((tile_rows + 8, wide, channels), bf16),
            pltpu.VMEM((tile_rows + 4, wide, channels), bf16),
            pltpu.VMEM((tile_rows + 4, wide, channels), bf16),
            pltpu.VMEM((tile_rows + 4, wide, channels), bf16),
            pltpu.VMEM((tile_rows, tile_cols, channels), f32),
            pltpu.VMEM((tile_rows, tile_cols, channels), f32),
            kernel_shape,
            kernel_shape,
            pltpu.VMEM((tile_rows, tile_cols, channels), bf16),
            pltpu.VMEM((2, width, channels), bf16),
        ]
        + [exchange] * 6
        + [table] * 4
        + [
            pltpu.VMEM((2, width, lanes), bf16),
            pltpu.VMEM((height, lanes), f32),
            pltpu.VMEM((lanes, depth), bf16),
            pltpu.VMEM((lanes, channels), bf16),
            pltpu.VMEM((lanes, lanes), bf16),
            pltpu.SemaphoreType.DMA((len(operands),)),
            pltpu.SemaphoreType.DMA((3, 8)),
            pltpu.SemaphoreType.DMA((3, 8)),
            pltpu.SemaphoreType.DMA((cols,)),
            pltpu.SemaphoreType.DMA((cols,)),
            pltpu.SemaphoreType.DMA((3,)),
            pltpu.SemaphoreType.DMA((3,)),
        ],
        compiler_params=pltpu.CompilerParams(
            collective_id=0, has_side_effects=True, vmem_limit_bytes=56 * 2**20
        ),
        name="block",
    )(*operands)
    total = jnp.einsum("rwc,cf->rwf", joined, weights, preferred_element_type=f32)
    return total.astype(bf16)


def solution(mesh):
    in_specs = (
        P("row", "col", None),
        P("row", "col", None),
        P("row", "col"),
        P(),
        P(),
        P(("row", "col"), None, None),
        P(),
        P(),
        P(),
        P(),
    )
    out_specs = P(("row", "col"), None, None)
    return jax.shard_map(shards, mesh=mesh, in_specs=in_specs, out_specs=out_specs, check_vma=False)
```

```python
import functools
import math

import jax
import jax.numpy as jnp
import numpy as np
from jax import lax
from jax.experimental import pallas as pl
from jax.experimental.pallas import tpu as pltpu
from jax.sharding import PartitionSpec as P

MESH = pl.DeviceIdType.MESH
SIDES = [(0, -1), (0, 1), (-1, 0), (1, 0), (-1, -1), (-1, 1), (1, -1), (1, 1)]
UNROLL = 8


def host_tables(length):
    ids = np.arange(length, dtype=np.int64)
    angles = (2.0 * np.pi / length) * ((ids[:, None] * ids[None, :]) % length)
    return (np.cos(angles).astype(jnp.bfloat16), np.sin(angles).astype(jnp.bfloat16))


def dot(left, right):
    return jnp.dot(left, right, preferred_element_type=jnp.float32)


def dot_t(left, right):
    return lax.dot_general(left, right, (((1,), (1,)), ((), ())), preferred_element_type=jnp.float32)


def ids(shape, dim):
    return lax.broadcasted_iota(jnp.int32, shape, dim)


def ones_where(condition):
    return jnp.where(condition, 1.0, 0.0).astype(jnp.bfloat16)


def block_kernel(
    sizes,
    features_any,
    target_any,
    mask_any,
    first_any,
    second_any,
    inputs_any,
    win_any,
    wout_any,
    wlocal_any,
    wmix_any,
    cos_any,
    sin_any,
    out_ref,
    target_ref,
    mask_ref,
    first_ref,
    second_ref,
    inputs_ref,
    win_ref,
    wout_ref,
    wlocal_ref,
    wmix_ref,
    cos_ref,
    sin_ref,
    feat_ext,
    act_ext,
    loss_ext,
    pre_ext,
    slope_first,
    hole_ref,
    first_adj,
    second_adj,
    grad_feat,
    strip_ref,
    spatial_out,
    spatial_in,
    grad_out,
    grad_in,
    back_out,
    back_in,
    col_cos,
    col_sin,
    col_cos_t,
    col_sin_t,
    held,
    slope_mix,
    win_double,
    wout_double,
    wmix_mixed,
    grad_local,
    load_sems,
    halo_send,
    halo_recv,
    strip_send,
    strip_recv,
    send_sems,
    recv_sems,
):
    rows, cols, height, width, chunks, tile_rows, tile_cols, channels, edge = sizes
    devices = rows * cols
    half_width = chunks * 64
    lanes = chunks * 128
    freqs = width // 2
    col_factor = 1.0 / math.sqrt(width)
    row_factor = 1.0 / math.sqrt(height)
    my_row = lax.axis_index("row")
    my_col = lax.axis_index("col")
    me = my_row * cols + my_col
    barrier = pltpu.get_barrier_semaphore()

    def each_peer(action, low=0, high=cols):
        for hop in range(low, high):
            col = lax.rem(my_col + hop, cols)
            per_turn = math.gcd(UNROLL, rows)

            def turn(index, carry, hop=hop, col=col):
                for k in range(per_turn):
                    action(lax.rem(my_row + (index * per_turn + k) * 21, rows), col)
                return carry

            if hop == 0:
                for k in range(1, per_turn):
                    action(lax.rem(my_row + k * 21, rows), col)
            lax.fori_loop(1 if hop == 0 else 0, rows // per_turn, turn, 0)

    def greet(row, col):
        pl.semaphore_signal(barrier, inc=1, device_id={"row": row, "col": col}, device_id_type=MESH)

    each_peer(greet)

    loads = [
        pltpu.make_async_copy(source, target, load_sems.at[index])
        for index, (source, target) in enumerate(
            [
                (win_any, win_ref),
                (inputs_any, inputs_ref),
                (cos_any, cos_ref),
                (sin_any, sin_ref),
                (first_any, first_ref),
                (second_any, second_ref),
                (features_any, feat_ext.at[pl.ds(4, tile_rows), pl.ds(edge, tile_cols)]),
                (wout_any, wout_ref),
                (wmix_any, wmix_ref),
                (mask_any, mask_ref),
                (target_any, target_ref),
                (wlocal_any, wlocal_ref),
            ]
        )
    ]
    for load in loads:
        load.start()

    def region(side, extent, thick, offset):
        if side < 0:
            return (offset, thick)
        if side > 0:
            return (offset + extent - thick, thick)
        return (offset, extent)

    def landing(side, extent, thick):
        if side < 0:
            return (extent + thick, thick)
        if side > 0:
            return (0, thick)
        return (thick, extent)

    def halo_copy(stage, side, source, target, thick, row_offset, col_offset):
        index = SIDES.index(side)
        source_rows = region(side[0], tile_rows, thick, row_offset)
        source_cols = region(side[1], tile_cols, edge, col_offset)
        target_rows = landing(side[0], tile_rows, thick)
        target_cols = landing(side[1], tile_cols, edge)
        return pltpu.make_async_remote_copy(
            src_ref=source.at[pl.ds(*source_rows), pl.ds(*source_cols)],
            dst_ref=target.at[pl.ds(*target_rows), pl.ds(*target_cols)],
            send_sem=halo_send.at[stage, index],
            recv_sem=halo_recv.at[stage, index],
            device_id={
                "row": lax.rem(my_row + side[0] + rows, rows),
                "col": lax.rem(my_col + side[1] + cols, cols),
            },
            device_id_type=MESH,
        )

    def exists(side, way):
        row, col = my_row + way * side[0], my_col + way * side[1]
        return (row >= 0) & (row < rows) & (col >= 0) & (col < cols)

    def begin(copies, indices):
        for index in indices:
            pl.when(exists(SIDES[index], 1))(copies[index].start)

    def receive(copies, indices):
        for index in indices:
            pl.when(exists(SIDES[index], -1))(copies[index].wait_recv)

    def flush(copies):
        for index in range(8):
            pl.when(exists(SIDES[index], 1))(copies[index].wait_send)

    def clear_rows(ext, thick):
        @pl.when(my_row == 0)
        def _():
            ext[0:thick] = jnp.zeros_like(ext[0:thick])

        @pl.when(my_row == rows - 1)
        def _():
            ext[thick + tile_rows :] = jnp.zeros_like(ext[thick + tile_rows :])

    def clear_cols(ext):
        @pl.when(my_col == 0)
        def _():
            ext[:, 0:edge] = jnp.zeros_like(ext[:, 0:edge])

        @pl.when(my_col == cols - 1)
        def _():
            ext[:, edge + tile_cols :] = jnp.zeros_like(ext[:, edge + tile_cols :])

    def conv_rows(ext, pieces, first_col, count, kernel):
        results = []
        for start, n in pieces:
            for row in range(start, start + n, 2):
                taps = [
                    ext[row + 2 * a : row + 2 * a + 2, first_col + 2 * b : first_col + 2 * b + count, :]
                    for a in range(3)
                    for b in range(3)
                ]
                joint = jnp.concatenate([tap.reshape(2 * count, channels) for tap in taps], axis=1)
                results.append((row, dot(joint, kernel[...]).reshape(2, count, channels)))
        return results

    for ext, thick in ((feat_ext, 4), (loss_ext, 2), (pre_ext, 2)):
        clear_rows(ext, thick)
        clear_cols(ext)

    even_row = ids((2 * freqs, 128), 0) % 2 == 0
    low_lane = ids((2 * freqs, 128), 1) < 64

    def column_forward(target):
        for j in range(chunks):
            piece = slice(j * 128, (j + 1) * 128)
            both = jnp.concatenate([held[0, :, piece], held[1, :, piece]], axis=1)
            cosine = dot(col_cos[...], both)
            sine = dot(col_sin[...], both)
            first = jnp.where(low_lane, cosine[:, :128], sine[:, :128])
            second = jnp.where(low_lane, cosine[:, 128:], sine[:, 128:])
            mixed_rows = (jnp.where(even_row, first, second) * col_factor).astype(jnp.bfloat16)
            target[j] = mixed_rows.reshape(freqs, 2, 128)

    def messages(source, target, index, low=0, high=cols):
        def send(row, col):
            pltpu.make_async_remote_copy(
                src_ref=source.at[:, row * cols + col],
                dst_ref=target.at[:, me],
                send_sem=send_sems.at[index],
                recv_sem=recv_sems.at[index],
                device_id={"row": row, "col": col},
                device_id_type=MESH,
            ).start()

        each_peer(send, low, high)
        if low == 0:
            pltpu.make_async_copy(source.at[:, me], target.at[:, me], recv_sems.at[index]).start()

    def arrived(target, index):
        pltpu.make_async_copy(target, target, recv_sems.at[index]).wait()

    def sent(source, index):
        rest = source.at[:, pl.ds(0, devices - 1)]
        pltpu.make_async_copy(rest, rest, send_sems.at[index]).wait()

    def row_transform(source, way):
        sign = jnp.where(ids((height, 128), 1) < 64, way, -way)
        results = []
        for j in range(chunks):
            cosine = dot(cos_ref[...], source[j])
            sine = dot(sin_ref[...], source[j])
            results.append((cosine + pltpu.roll(sine, 64, 1) * sign) * row_factor)
        return results

    pl.semaphore_wait(barrier, devices - 1)
    features_out = [halo_copy(0, side, features_any, feat_ext, 4, 0, 0) for side in SIDES]
    begin(features_out, range(8))

    loads[0].wait()
    double_t = ones_where(ids((lanes, half_width), 1) == 64 * (ids((lanes, half_width), 0) // 128) + ids((lanes, half_width), 0) % 64)
    win_double[...] = dot(double_t, win_ref[...]).astype(jnp.bfloat16)
    loads[1].wait()
    for i in range(2):
        held[i] = dot_t(inputs_ref[i], win_double[...]).astype(jnp.bfloat16)
    loads[2].wait()
    loads[3].wait()
    pick = ones_where(ids((2 * freqs, freqs), 0) // 2 == ids((2 * freqs, freqs), 1))
    pick_t = ones_where(ids((freqs, 2 * freqs), 1) // 2 == ids((freqs, 2 * freqs), 0))
    alternate = (1 - 2 * (ids((2 * freqs, width), 1) % 2)).astype(jnp.float32)
    alternate_t = (1 - 2 * (ids((width, 2 * freqs), 0) % 2)).astype(jnp.float32)
    col_cos[...] = dot(pick, cos_ref[:freqs, :]).astype(jnp.bfloat16)
    col_sin[...] = jnp.where(ids((2 * freqs, width), 0) < 2, alternate, -dot(pick, sin_ref[:freqs, :])).astype(jnp.bfloat16)
    column_forward(spatial_out)
    loads[4].wait()
    receive(features_out, (0, 1))
    loads[6].wait()

    wide = tile_cols + edge
    margin = edge // 2

    def first_conv(start):
        shape = (2, wide, channels)
        for row, pre in conv_rows(feat_ext, [(start, 4)], edge - margin - 2, wide, first_ref):
            gate = jax.nn.sigmoid(pre)
            row_id = my_row * tile_rows - 2 + row + ids(shape, 0)
            col_id = my_col * tile_cols - margin + ids(shape, 1)
            inside = (row_id >= 0) & (row_id < height) & (col_id >= 0) & (col_id < width)
            act = jnp.where(inside, pre * gate, 0.0).astype(jnp.bfloat16)
            act_ext[row : row + 2, edge - margin : edge - margin + wide, :] = act
            if 2 <= row < 2 + tile_rows:
                slope = gate * (1.0 + pre * (1.0 - gate))
                slope_first[row - 2 : row] = slope[:, margin : margin + tile_cols, :]

    first_conv(4)

    loads[5].wait()
    eye = ones_where(ids((channels, channels), 0) == ids((channels, channels), 1))
    for source, target in ((first_ref, first_adj), (second_ref, second_adj)):
        for tap in range(9):
            block = source[(8 - tap) * channels : (9 - tap) * channels, :]
            target[tap * channels : (tap + 1) * channels, :] = dot_t(eye, block).astype(jnp.bfloat16)
    loads[9].wait()
    spot = ids((tile_cols, tile_cols), 0) == ids((tile_cols, tile_cols), 1)
    for p in range(tile_rows):
        line = mask_ref[p : p + 1, :].astype(jnp.float32)
        spread = jnp.where(spot, line, 0.0).astype(jnp.bfloat16)
        hole_ref[p] = 1.0 + 2.0 * dot(spread, jnp.ones((tile_cols, channels), jnp.bfloat16))
    receive(features_out, range(2, 8))
    messages(spatial_out, spatial_in, 0, 0, 1)
    first_conv(0)
    first_conv(8)

    outer = [(0, 2), (tile_rows - 2, 2)]
    inner = [(2, tile_rows - 4)]

    body = slice(edge, edge + tile_cols)

    def second_conv(pieces):
        for row, pre in conv_rows(act_ext, pieces, edge - 2, tile_cols, second_ref):
            loss = hole_ref[row : row + 2] * (pre - target_ref[row : row + 2].astype(jnp.float32))
            loss_ext[row + 2 : row + 4, body, :] = loss.astype(jnp.bfloat16)

    loads[10].wait()
    loss_out = [halo_copy(1, side, loss_ext, loss_ext, 2, 2, edge) for side in SIDES]
    second_conv(outer)
    begin(loss_out, range(2, 8))
    second_conv(inner)
    begin(loss_out, (0, 1))
    receive(loss_out, (0, 1))

    def third_conv(pieces):
        for row, value in conv_rows(loss_ext, pieces, edge - 2, tile_cols, second_adj):
            pre_ext[row + 2 : row + 4, body, :] = (value * slope_first[row : row + 2]).astype(jnp.bfloat16)

    third_conv(inner)
    receive(loss_out, range(2, 8))
    messages(spatial_out, spatial_in, 0, 1, 2)
    pre_out = [halo_copy(2, side, pre_ext, pre_ext, 2, 2, edge) for side in SIDES]
    third_conv(outer)
    begin(pre_out, range(8))

    col_cos_t[...] = dot(cos_ref[:, :freqs], pick_t).astype(jnp.bfloat16)
    col_sin_t[...] = jnp.where(ids((width, 2 * freqs), 1) < 2, alternate_t, -dot(sin_ref[:, :freqs], pick_t)).astype(jnp.bfloat16)
    loads[7].wait()
    wout_double[...] = dot(double_t, wout_ref[...]).astype(jnp.bfloat16)

    def place_of(lane):
        return ((lane % 128) // 64) * half_width + 64 * (lane // 128) + lane % 64

    order = ones_where(ids((lanes, lanes), 0) == place_of(ids((lanes, lanes), 1)))
    order_t = ones_where(ids((lanes, lanes), 1) == place_of(ids((lanes, lanes), 0)))
    loads[8].wait()
    partly = dot(order_t, wmix_ref[...]).astype(jnp.bfloat16)
    wmix_mixed[...] = dot(partly, order).astype(jnp.bfloat16)
    loads[11].wait()
    low_half = ids(win_double.shape, 0) % 128 < 64
    win_double[...] = jnp.where(low_half, win_double[...].astype(jnp.float32), 0.0).astype(jnp.bfloat16)
    receive(pre_out, (0, 1))

    def fourth_conv(pieces):
        for row, value in conv_rows(pre_ext, pieces, edge - 2, tile_cols, first_adj):
            grad_feat[row : row + 2] = value.astype(jnp.bfloat16)

    here = pl.ds(pl.multiple_of(my_col * tile_cols, tile_cols), tile_cols)

    def strip_copy(peer_col):
        return pltpu.make_async_remote_copy(
            src_ref=grad_feat.at[pl.ds(2 * peer_col, 2)],
            dst_ref=strip_ref.at[:, here],
            send_sem=strip_send.at[peer_col],
            recv_sem=strip_recv.at[my_col],
            device_id={"row": my_row, "col": peer_col},
            device_id_type=MESH,
        )

    def strip_own():
        return pltpu.make_async_copy(
            grad_feat.at[pl.ds(2 * my_col, 2)], strip_ref.at[:, here], strip_recv.at[my_col]
        )

    def strip_begin(peer_cols):
        for peer_col in peer_cols:
            pl.when(my_col != peer_col)(strip_copy(peer_col).start)
            pl.when(my_col == peer_col)(strip_own().start)

    def strip_receive():
        for peer_col in range(cols):
            part = strip_ref.at[:, pl.ds(peer_col * tile_cols, tile_cols)]
            pltpu.make_async_copy(part, part, strip_recv.at[peer_col]).wait()

    fourth_conv(inner)
    strip_begin(range(1, cols - 1))
    receive(pre_out, range(2, 8))
    messages(spatial_out, spatial_in, 0, 2, cols)
    fourth_conv(outer)
    strip_begin((0, cols - 1))

    strip_receive()
    for i in range(2):
        held[i] = dot_t(strip_ref[i], wout_double[...]).astype(jnp.bfloat16)
    column_forward(grad_out)
    messages(grad_out, grad_in, 1)

    arrived(spatial_in, 0)
    freq = row_transform([spatial_in[j].reshape(height, 128) for j in range(chunks)], 1.0)
    pre_mix = dot(jnp.concatenate(freq, axis=1).astype(jnp.bfloat16), wmix_mixed[...])
    gate = jax.nn.sigmoid(pre_mix)
    slope_mix[...] = gate * (1.0 + pre_mix * (1.0 - gate))

    arrived(grad_in, 1)
    freq = row_transform([grad_in[j].reshape(height, 128) for j in range(chunks)], 1.0)
    grad_mix = (jnp.concatenate(freq, axis=1) * slope_mix[...]).astype(jnp.bfloat16)
    mixed = dot_t(grad_mix, wmix_mixed[...]).astype(jnp.bfloat16)
    back = row_transform([mixed[:, j * 128 : (j + 1) * 128] for j in range(chunks)], -1.0)
    for j in range(chunks):
        back_out[j] = back[j].astype(jnp.bfloat16).reshape(devices, 2, 128)
    messages(back_out, back_in, 2)
    for copies in (features_out, loss_out, pre_out):
        flush(copies)
    for peer_col in range(cols):
        pl.when(my_col != peer_col)(strip_copy(peer_col).wait_send)
    sent(spatial_out, 0)
    sent(grad_out, 1)
    for i in range(2):
        grad_local[i] = dot_t(strip_ref[i], wlocal_ref[...])
    arrived(back_in, 2)
    keep = ids((width, 128), 1) < 64
    for j in range(chunks):
        block = back_in[j].reshape(2 * freqs, 128).astype(jnp.float32)
        both = jnp.concatenate([jnp.where(even_row, block, 0.0), jnp.where(even_row, 0.0, block)], axis=1)
        both = both.astype(jnp.bfloat16)
        cosine = dot(col_cos_t[...], both)
        sine = dot(col_sin_t[...], both)
        for i in range(2):
            piece = slice(i * 128, (i + 1) * 128)
            total = (cosine[:, piece] + pltpu.roll(sine[:, piece], 64, 1)) * col_factor
            held[i, :, j * 128 : (j + 1) * 128] = jnp.where(keep, total, 0.0).astype(jnp.bfloat16)
    for i in range(2):
        out_ref[i] = (dot(held[i], win_double[...]) + grad_local[i]).astype(jnp.bfloat16)
    sent(back_out, 2)


def shards(
    features,
    target,
    hole_mask,
    kernel_first,
    kernel_second,
    inputs,
    weight_in,
    weight_out,
    weight_local,
    weight_mix,
):
    rows, cols = lax.axis_size("row"), lax.axis_size("col")
    devices = rows * cols
    tile_rows, tile_cols, channels = features.shape
    width = inputs.shape[1]
    height = inputs.shape[0] * devices
    depth = inputs.shape[2]
    chunks = weight_in.shape[1] // 64
    lanes = chunks * 128
    edge = min(16, tile_cols)
    cos_table, sin_table = host_tables(width)
    wide = tile_cols + 2 * edge
    bf16, f32 = jnp.bfloat16, jnp.float32
    operands = (
        features,
        target,
        hole_mask,
        kernel_first.reshape(9 * channels, channels),
        kernel_second.reshape(9 * channels, channels),
        inputs,
        weight_in.T,
        weight_out,
        weight_local,
        weight_mix,
        jnp.asarray(cos_table),
        jnp.asarray(sin_table),
    )
    exchange = pltpu.VMEM((chunks, devices, 2, 128), bf16)
    table = pltpu.VMEM((width, width), bf16)
    kernel_shape = pltpu.VMEM((9 * channels, channels), bf16)
    vmem = pl.BlockSpec(memory_space=pltpu.VMEM)
    return pl.pallas_call(
        functools.partial(
            block_kernel, (rows, cols, height, width, chunks, tile_rows, tile_cols, channels, edge)
        ),
        out_shape=jax.ShapeDtypeStruct((2, width, depth), bf16),
        in_specs=[pl.BlockSpec(memory_space=pl.ANY)] * len(operands),
        out_specs=vmem,
        scratch_shapes=[pltpu.VMEM(item.shape, item.dtype) for item in operands[1:]]
        + [
            pltpu.VMEM((tile_rows + 8, wide, channels), bf16),
            pltpu.VMEM((tile_rows + 4, wide, channels), bf16),
            pltpu.VMEM((tile_rows + 4, wide, channels), bf16),
            pltpu.VMEM((tile_rows + 4, wide, channels), bf16),
            pltpu.VMEM((tile_rows, tile_cols, channels), f32),
            pltpu.VMEM((tile_rows, tile_cols, channels), f32),
            kernel_shape,
            kernel_shape,
            pltpu.VMEM((tile_rows, tile_cols, channels), bf16),
            pltpu.VMEM((2, width, channels), bf16),
        ]
        + [exchange] * 6
        + [table] * 4
        + [
            pltpu.VMEM((2, width, lanes), bf16),
            pltpu.VMEM((height, lanes), f32),
            pltpu.VMEM((lanes, depth), bf16),
            pltpu.VMEM((lanes, channels), bf16),
            pltpu.VMEM((lanes, lanes), bf16),
            pltpu.VMEM((2, width, depth), f32),
            pltpu.SemaphoreType.DMA((len(operands),)),
            pltpu.SemaphoreType.DMA((3, 8)),
            pltpu.SemaphoreType.DMA((3, 8)),
            pltpu.SemaphoreType.DMA((cols,)),
            pltpu.SemaphoreType.DMA((cols,)),
            pltpu.SemaphoreType.DMA((3,)),
            pltpu.SemaphoreType.DMA((3,)),
        ],
        compiler_params=pltpu.CompilerParams(
            collective_id=0, has_side_effects=True, vmem_limit_bytes=56 * 2**20
        ),
        name="block",
    )(*operands)


def solution(mesh):
    in_specs = (
        P("row", "col", None),
        P("row", "col", None),
        P("row", "col"),
        P(),
        P(),
        P(("row", "col"), None, None),
        P(),
        P(),
        P(),
        P(),
    )
    out_specs = P(("row", "col"), None, None)
    return jax.shard_map(shards, mesh=mesh, in_specs=in_specs, out_specs=out_specs, check_vma=False)
```

```python
import functools
import math

import jax
import jax.numpy as jnp
import numpy as np
from jax import lax
from jax.experimental import pallas as pl
from jax.experimental.pallas import tpu as pltpu
from jax.sharding import PartitionSpec as P

MESH = pl.DeviceIdType.MESH
SIDES = [(0, -1), (0, 1), (-1, 0), (1, 0), (-1, -1), (-1, 1), (1, -1), (1, 1)]
UNROLL = 8


def host_tables(length):
    ids = np.arange(length, dtype=np.int64)
    angles = (2.0 * np.pi / length) * ((ids[:, None] * ids[None, :]) % length)
    return (np.cos(angles).astype(jnp.bfloat16), np.sin(angles).astype(jnp.bfloat16))


def dot(left, right):
    return jnp.dot(left, right, preferred_element_type=jnp.float32)


def dot_t(left, right):
    return lax.dot_general(left, right, (((1,), (1,)), ((), ())), preferred_element_type=jnp.float32)


def ids(shape, dim):
    return lax.broadcasted_iota(jnp.int32, shape, dim)


def ones_where(condition):
    return jnp.where(condition, 1.0, 0.0).astype(jnp.bfloat16)


def block_kernel(
    sizes,
    features_any,
    target_any,
    mask_any,
    first_any,
    second_any,
    inputs_any,
    win_any,
    wout_any,
    wlocal_any,
    wmix_any,
    cos_any,
    sin_any,
    out_ref,
    target_ref,
    mask_ref,
    first_ref,
    second_ref,
    inputs_ref,
    win_ref,
    wout_ref,
    wlocal_ref,
    wmix_ref,
    cos_ref,
    sin_ref,
    feat_ext,
    act_ext,
    loss_ext,
    pre_ext,
    slope_first,
    hole_ref,
    first_adj,
    second_adj,
    grad_feat,
    strip_ref,
    spatial_out,
    spatial_in,
    grad_out,
    grad_in,
    back_out,
    back_in,
    col_cos,
    col_sin,
    col_cos_t,
    col_sin_t,
    held,
    slope_mix,
    win_double,
    wout_double,
    wmix_mixed,
    grad_local,
    relay_feat,
    relay_loss,
    relay_pre,
    relay_sems,
    load_sems,
    halo_send,
    halo_recv,
    strip_send,
    strip_recv,
    send_sems,
    recv_sems,
):
    rows, cols, height, width, chunks, tile_rows, tile_cols, channels, edge = sizes
    devices = rows * cols
    half_width = chunks * 64
    lanes = chunks * 128
    freqs = width // 2
    col_factor = 1.0 / math.sqrt(width)
    row_factor = 1.0 / math.sqrt(height)
    my_row = lax.axis_index("row")
    my_col = lax.axis_index("col")
    me = my_row * cols + my_col
    barrier = pltpu.get_barrier_semaphore()

    def each_peer(action, low=0, high=cols):
        for hop in range(low, high):
            col = lax.rem(my_col + hop, cols)
            per_turn = math.gcd(UNROLL, rows)

            def turn(index, carry, hop=hop, col=col):
                for k in range(per_turn):
                    action(lax.rem(my_row + (index * per_turn + k) * 21, rows), col)
                return carry

            if hop == 0:
                for k in range(1, per_turn):
                    action(lax.rem(my_row + k * 21, rows), col)
            lax.fori_loop(1 if hop == 0 else 0, rows // per_turn, turn, 0)

    def greet(row, col):
        pl.semaphore_signal(barrier, inc=1, device_id={"row": row, "col": col}, device_id_type=MESH)

    each_peer(greet)

    loads = [
        pltpu.make_async_copy(source, target, load_sems.at[index])
        for index, (source, target) in enumerate(
            [
                (win_any, win_ref),
                (inputs_any, inputs_ref),
                (cos_any, cos_ref),
                (sin_any, sin_ref),
                (first_any, first_ref),
                (second_any, second_ref),
                (features_any, feat_ext.at[pl.ds(4, tile_rows), pl.ds(edge, tile_cols)]),
                (wout_any, wout_ref),
                (wmix_any, wmix_ref),
                (mask_any, mask_ref),
                (target_any, target_ref),
                (wlocal_any, wlocal_ref),
            ]
        )
    ]
    for load in loads:
        load.start()

    def region(side, extent, thick, offset):
        if side < 0:
            return (offset, thick)
        if side > 0:
            return (offset + extent - thick, thick)
        return (offset, extent)

    def landing(side, extent, thick):
        if side < 0:
            return (extent + thick, thick)
        if side > 0:
            return (0, thick)
        return (thick, extent)

    group = 4 if rows % 16 == 0 else 2
    split = tile_cols * 5 // 8
    rest = tile_cols - split
    in_group = lax.rem(my_row, group)
    at_first, at_last = in_group == 0, in_group == group - 1

    def halo_copy(stage, side, source, target, thick, row_offset, col_offset, part=False):
        index = SIDES.index(side)
        source_rows = region(side[0], tile_rows, thick, row_offset)
        source_cols = region(side[1], tile_cols, edge, col_offset)
        target_rows = landing(side[0], tile_rows, thick)
        target_cols = landing(side[1], tile_cols, edge)
        if part:
            source_cols, target_cols = (col_offset, split), (edge, split)
        return pltpu.make_async_remote_copy(
            src_ref=source.at[pl.ds(*source_rows), pl.ds(*source_cols)],
            dst_ref=target.at[pl.ds(*target_rows), pl.ds(*target_cols)],
            send_sem=halo_send.at[stage, index],
            recv_sem=halo_recv.at[stage, index],
            device_id={
                "row": lax.rem(my_row + side[0] + rows, rows),
                "col": lax.rem(my_col + side[1] + cols, cols),
            },
            device_id_type=MESH,
        )

    def exists(side, way):
        row, col = my_row + way * side[0], my_col + way * side[1]
        return (row >= 0) & (row < rows) & (col >= 0) & (col < cols)

    class Exchange:
        def __init__(self, stage, source, target, thick, row_offset, col_offset, buffer):
            common = (source, target, thick, row_offset, col_offset)
            self.whole = [halo_copy(stage, side, *common) for side in SIDES]
            self.part = {index: halo_copy(stage, SIDES[index], *common, part=True) for index in (2, 3)}

            def hop(row_start, distance):
                return pltpu.make_async_remote_copy(
                    src_ref=source.at[pl.ds(row_start, thick), pl.ds(col_offset + split, rest)],
                    dst_ref=buffer,
                    send_sem=relay_sems.at[0, stage],
                    recv_sem=relay_sems.at[1, stage],
                    device_id={"row": lax.rem(my_row + distance + rows, rows), "col": my_col},
                    device_id_type=MESH,
                )

            def onward(row_start, distance):
                return pltpu.make_async_remote_copy(
                    src_ref=buffer,
                    dst_ref=target.at[pl.ds(row_start, thick), pl.ds(edge + split, rest)],
                    send_sem=relay_sems.at[2, stage],
                    recv_sem=relay_sems.at[3, stage],
                    device_id={"row": lax.rem(my_row + distance + rows, rows), "col": my_col},
                    device_id_type=MESH,
                )

            back, ahead = my_row >= group, my_row + group < rows
            up = hop(row_offset, group - 1)
            down = hop(row_offset + tile_rows - thick, 1 - group)
            self.hops = [(at_first & back, up), (at_last & ahead, down)]
            self.onwards = [
                (at_first & ahead, onward(0, group)),
                (at_last & back, onward(thick + tile_rows, -group)),
            ]
            self.finals = [
                (at_first & back, onward(0, group)),
                (at_last & ahead, onward(thick + tile_rows, -group)),
            ]

        def each(self, index, way, action):
            there = exists(SIDES[index], way)
            if index not in (2, 3):
                pl.when(there)(getattr(self.whole[index], action))
                return
            far = at_first if (SIDES[index][0] < 0) == (way > 0) else at_last
            pl.when(there & far)(getattr(self.part[index], action))
            pl.when(there & jnp.logical_not(far))(getattr(self.whole[index], action))

        def begin(self, indices):
            if 2 in indices:
                for there, copy in self.hops:
                    pl.when(there)(copy.start)
            for index in indices:
                self.each(index, 1, "start")

        def relay(self):
            for there, copy in self.onwards:

                @pl.when(there)
                def _(copy=copy):
                    self.hops[0][1].wait_recv()
                    copy.start()

        def receive(self, indices):
            for index in indices:
                self.each(index, -1, "wait_recv")
            if 2 in indices:
                for there, copy in self.finals:
                    pl.when(there)(copy.wait_recv)

        def flush(self):
            for index in range(8):
                self.each(index, 1, "wait_send")
            for there, copy in self.hops + self.onwards:
                pl.when(there)(copy.wait_send)

    def clear_rows(ext, thick):
        @pl.when(my_row == 0)
        def _():
            ext[0:thick] = jnp.zeros_like(ext[0:thick])

        @pl.when(my_row == rows - 1)
        def _():
            ext[thick + tile_rows :] = jnp.zeros_like(ext[thick + tile_rows :])

    def clear_cols(ext):
        @pl.when(my_col == 0)
        def _():
            ext[:, 0:edge] = jnp.zeros_like(ext[:, 0:edge])

        @pl.when(my_col == cols - 1)
        def _():
            ext[:, edge + tile_cols :] = jnp.zeros_like(ext[:, edge + tile_cols :])

    def conv_rows(ext, pieces, first_col, count, kernel):
        results = []
        for start, n in pieces:
            for row in range(start, start + n, 2):
                taps = [
                    ext[row + 2 * a : row + 2 * a + 2, first_col + 2 * b : first_col + 2 * b + count, :]
                    for a in range(3)
                    for b in range(3)
                ]
                joint = jnp.concatenate([tap.reshape(2 * count, channels) for tap in taps], axis=1)
                results.append((row, dot(joint, kernel[...]).reshape(2, count, channels)))
        return results

    for ext, thick in ((feat_ext, 4), (loss_ext, 2), (pre_ext, 2)):
        clear_rows(ext, thick)
        clear_cols(ext)

    even_row = ids((2 * freqs, 128), 0) % 2 == 0
    low_lane = ids((2 * freqs, 128), 1) < 64

    def column_forward(target):
        for j in range(chunks):
            piece = slice(j * 128, (j + 1) * 128)
            both = jnp.concatenate([held[0, :, piece], held[1, :, piece]], axis=1)
            cosine = dot(col_cos[...], both)
            sine = dot(col_sin[...], both)
            first = jnp.where(low_lane, cosine[:, :128], sine[:, :128])
            second = jnp.where(low_lane, cosine[:, 128:], sine[:, 128:])
            mixed_rows = (jnp.where(even_row, first, second) * col_factor).astype(jnp.bfloat16)
            target[j] = mixed_rows.reshape(freqs, 2, 128)

    def messages(source, target, index, low=0, high=cols):
        def send(row, col):
            pltpu.make_async_remote_copy(
                src_ref=source.at[:, row * cols + col],
                dst_ref=target.at[:, me],
                send_sem=send_sems.at[index],
                recv_sem=recv_sems.at[index],
                device_id={"row": row, "col": col},
                device_id_type=MESH,
            ).start()

        each_peer(send, low, high)
        if low == 0:
            pltpu.make_async_copy(source.at[:, me], target.at[:, me], recv_sems.at[index]).start()

    def arrived(target, index):
        pltpu.make_async_copy(target, target, recv_sems.at[index]).wait()

    def sent(source, index):
        rest = source.at[:, pl.ds(0, devices - 1)]
        pltpu.make_async_copy(rest, rest, send_sems.at[index]).wait()

    def row_transform(source, way):
        sign = jnp.where(ids((height, 128), 1) < 64, way, -way)
        results = []
        for j in range(chunks):
            cosine = dot(cos_ref[...], source[j])
            sine = dot(sin_ref[...], source[j])
            results.append((cosine + pltpu.roll(sine, 64, 1) * sign) * row_factor)
        return results

    pl.semaphore_wait(barrier, devices - 1)
    features_out = Exchange(0, features_any, feat_ext, 4, 0, 0, relay_feat)
    features_out.begin(range(8))

    loads[0].wait()
    double_t = ones_where(ids((lanes, half_width), 1) == 64 * (ids((lanes, half_width), 0) // 128) + ids((lanes, half_width), 0) % 64)
    win_double[...] = dot(double_t, win_ref[...]).astype(jnp.bfloat16)
    loads[1].wait()
    for i in range(2):
        held[i] = dot_t(inputs_ref[i], win_double[...]).astype(jnp.bfloat16)
    loads[2].wait()
    loads[3].wait()
    pick = ones_where(ids((2 * freqs, freqs), 0) // 2 == ids((2 * freqs, freqs), 1))
    pick_t = ones_where(ids((freqs, 2 * freqs), 1) // 2 == ids((freqs, 2 * freqs), 0))
    alternate = (1 - 2 * (ids((2 * freqs, width), 1) % 2)).astype(jnp.float32)
    alternate_t = (1 - 2 * (ids((width, 2 * freqs), 0) % 2)).astype(jnp.float32)
    col_cos[...] = dot(pick, cos_ref[:freqs, :]).astype(jnp.bfloat16)
    col_sin[...] = jnp.where(ids((2 * freqs, width), 0) < 2, alternate, -dot(pick, sin_ref[:freqs, :])).astype(jnp.bfloat16)
    column_forward(spatial_out)
    loads[4].wait()
    features_out.receive((0, 1))
    features_out.relay()
    loads[6].wait()

    wide = tile_cols + edge
    margin = edge // 2

    def first_conv(start):
        shape = (2, wide, channels)
        for row, pre in conv_rows(feat_ext, [(start, 4)], edge - margin - 2, wide, first_ref):
            gate = jax.nn.sigmoid(pre)
            row_id = my_row * tile_rows - 2 + row + ids(shape, 0)
            col_id = my_col * tile_cols - margin + ids(shape, 1)
            inside = (row_id >= 0) & (row_id < height) & (col_id >= 0) & (col_id < width)
            act = jnp.where(inside, pre * gate, 0.0).astype(jnp.bfloat16)
            act_ext[row : row + 2, edge - margin : edge - margin + wide, :] = act
            if 2 <= row < 2 + tile_rows:
                slope = gate * (1.0 + pre * (1.0 - gate))
                slope_first[row - 2 : row] = slope[:, margin : margin + tile_cols, :]

    first_conv(4)

    loads[5].wait()
    eye = ones_where(ids((channels, channels), 0) == ids((channels, channels), 1))
    for source, target in ((first_ref, first_adj), (second_ref, second_adj)):
        for tap in range(9):
            block = source[(8 - tap) * channels : (9 - tap) * channels, :]
            target[tap * channels : (tap + 1) * channels, :] = dot_t(eye, block).astype(jnp.bfloat16)
    loads[9].wait()
    spot = ids((tile_cols, tile_cols), 0) == ids((tile_cols, tile_cols), 1)
    for p in range(tile_rows):
        line = mask_ref[p : p + 1, :].astype(jnp.float32)
        spread = jnp.where(spot, line, 0.0).astype(jnp.bfloat16)
        hole_ref[p] = 1.0 + 2.0 * dot(spread, jnp.ones((tile_cols, channels), jnp.bfloat16))
    features_out.receive(range(2, 8))
    messages(spatial_out, spatial_in, 0, 0, 1)
    first_conv(0)
    first_conv(8)

    outer = [(0, 2), (tile_rows - 2, 2)]
    inner = [(2, tile_rows - 4)]

    body = slice(edge, edge + tile_cols)

    def second_conv(pieces):
        for row, pre in conv_rows(act_ext, pieces, edge - 2, tile_cols, second_ref):
            loss = hole_ref[row : row + 2] * (pre - target_ref[row : row + 2].astype(jnp.float32))
            loss_ext[row + 2 : row + 4, body, :] = loss.astype(jnp.bfloat16)

    loads[10].wait()
    loss_out = Exchange(1, loss_ext, loss_ext, 2, 2, edge, relay_loss)
    second_conv(outer)
    loss_out.begin(range(2, 8))
    second_conv(inner)
    loss_out.begin((0, 1))
    loss_out.receive((0, 1))
    loss_out.relay()

    def third_conv(pieces):
        for row, value in conv_rows(loss_ext, pieces, edge - 2, tile_cols, second_adj):
            pre_ext[row + 2 : row + 4, body, :] = (value * slope_first[row : row + 2]).astype(jnp.bfloat16)

    third_conv(inner)
    loss_out.receive(range(2, 8))
    messages(spatial_out, spatial_in, 0, 1, 2)
    pre_out = Exchange(2, pre_ext, pre_ext, 2, 2, edge, relay_pre)
    third_conv(outer)
    pre_out.begin(range(8))

    col_cos_t[...] = dot(cos_ref[:, :freqs], pick_t).astype(jnp.bfloat16)
    col_sin_t[...] = jnp.where(ids((width, 2 * freqs), 1) < 2, alternate_t, -dot(sin_ref[:, :freqs], pick_t)).astype(jnp.bfloat16)
    loads[7].wait()
    wout_double[...] = dot(double_t, wout_ref[...]).astype(jnp.bfloat16)

    def place_of(lane):
        return ((lane % 128) // 64) * half_width + 64 * (lane // 128) + lane % 64

    order = ones_where(ids((lanes, lanes), 0) == place_of(ids((lanes, lanes), 1)))
    order_t = ones_where(ids((lanes, lanes), 1) == place_of(ids((lanes, lanes), 0)))
    loads[8].wait()
    partly = dot(order_t, wmix_ref[...]).astype(jnp.bfloat16)
    wmix_mixed[...] = dot(partly, order).astype(jnp.bfloat16)
    loads[11].wait()
    low_half = ids(win_double.shape, 0) % 128 < 64
    win_double[...] = jnp.where(low_half, win_double[...].astype(jnp.float32), 0.0).astype(jnp.bfloat16)
    pre_out.receive((0, 1))
    pre_out.relay()

    def fourth_conv(pieces):
        for row, value in conv_rows(pre_ext, pieces, edge - 2, tile_cols, first_adj):
            grad_feat[row : row + 2] = value.astype(jnp.bfloat16)

    here = pl.ds(pl.multiple_of(my_col * tile_cols, tile_cols), tile_cols)

    def strip_copy(peer_col):
        return pltpu.make_async_remote_copy(
            src_ref=grad_feat.at[pl.ds(2 * peer_col, 2)],
            dst_ref=strip_ref.at[:, here],
            send_sem=strip_send.at[peer_col],
            recv_sem=strip_recv.at[my_col],
            device_id={"row": my_row, "col": peer_col},
            device_id_type=MESH,
        )

    def strip_own():
        return pltpu.make_async_copy(
            grad_feat.at[pl.ds(2 * my_col, 2)], strip_ref.at[:, here], strip_recv.at[my_col]
        )

    def strip_begin(peer_cols):
        for peer_col in peer_cols:
            pl.when(my_col != peer_col)(strip_copy(peer_col).start)
            pl.when(my_col == peer_col)(strip_own().start)

    def strip_receive():
        for peer_col in range(cols):
            part = strip_ref.at[:, pl.ds(peer_col * tile_cols, tile_cols)]
            pltpu.make_async_copy(part, part, strip_recv.at[peer_col]).wait()

    fourth_conv(inner)
    strip_begin(range(1, cols - 1))
    pre_out.receive(range(2, 8))
    messages(spatial_out, spatial_in, 0, 2, cols)
    fourth_conv(outer)
    strip_begin((0, cols - 1))

    strip_receive()
    for i in range(2):
        held[i] = dot_t(strip_ref[i], wout_double[...]).astype(jnp.bfloat16)
    column_forward(grad_out)
    messages(grad_out, grad_in, 1)

    arrived(spatial_in, 0)
    freq = row_transform([spatial_in[j].reshape(height, 128) for j in range(chunks)], 1.0)
    pre_mix = dot(jnp.concatenate(freq, axis=1).astype(jnp.bfloat16), wmix_mixed[...])
    gate = jax.nn.sigmoid(pre_mix)
    slope_mix[...] = gate * (1.0 + pre_mix * (1.0 - gate))

    arrived(grad_in, 1)
    freq = row_transform([grad_in[j].reshape(height, 128) for j in range(chunks)], 1.0)
    grad_mix = (jnp.concatenate(freq, axis=1) * slope_mix[...]).astype(jnp.bfloat16)
    mixed = dot_t(grad_mix, wmix_mixed[...]).astype(jnp.bfloat16)
    back = row_transform([mixed[:, j * 128 : (j + 1) * 128] for j in range(chunks)], -1.0)
    for j in range(chunks):
        back_out[j] = back[j].astype(jnp.bfloat16).reshape(devices, 2, 128)
    messages(back_out, back_in, 2)
    for exchange in (features_out, loss_out, pre_out):
        exchange.flush()
    for peer_col in range(cols):
        pl.when(my_col != peer_col)(strip_copy(peer_col).wait_send)
    sent(spatial_out, 0)
    sent(grad_out, 1)
    for i in range(2):
        grad_local[i] = dot_t(strip_ref[i], wlocal_ref[...])
    arrived(back_in, 2)
    keep = ids((width, 128), 1) < 64
    for j in range(chunks):
        block = back_in[j].reshape(2 * freqs, 128).astype(jnp.float32)
        both = jnp.concatenate([jnp.where(even_row, block, 0.0), jnp.where(even_row, 0.0, block)], axis=1)
        both = both.astype(jnp.bfloat16)
        cosine = dot(col_cos_t[...], both)
        sine = dot(col_sin_t[...], both)
        for i in range(2):
            piece = slice(i * 128, (i + 1) * 128)
            total = (cosine[:, piece] + pltpu.roll(sine[:, piece], 64, 1)) * col_factor
            held[i, :, j * 128 : (j + 1) * 128] = jnp.where(keep, total, 0.0).astype(jnp.bfloat16)
    for i in range(2):
        out_ref[i] = (dot(held[i], win_double[...]) + grad_local[i]).astype(jnp.bfloat16)
    sent(back_out, 2)


def shards(
    features,
    target,
    hole_mask,
    kernel_first,
    kernel_second,
    inputs,
    weight_in,
    weight_out,
    weight_local,
    weight_mix,
):
    rows, cols = lax.axis_size("row"), lax.axis_size("col")
    devices = rows * cols
    tile_rows, tile_cols, channels = features.shape
    width = inputs.shape[1]
    height = inputs.shape[0] * devices
    depth = inputs.shape[2]
    chunks = weight_in.shape[1] // 64
    lanes = chunks * 128
    edge = min(16, tile_cols)
    cos_table, sin_table = host_tables(width)
    wide = tile_cols + 2 * edge
    bf16, f32 = jnp.bfloat16, jnp.float32
    operands = (
        features,
        target,
        hole_mask,
        kernel_first.reshape(9 * channels, channels),
        kernel_second.reshape(9 * channels, channels),
        inputs,
        weight_in.T,
        weight_out,
        weight_local,
        weight_mix,
        jnp.asarray(cos_table),
        jnp.asarray(sin_table),
    )
    exchange = pltpu.VMEM((chunks, devices, 2, 128), bf16)
    table = pltpu.VMEM((width, width), bf16)
    kernel_shape = pltpu.VMEM((9 * channels, channels), bf16)
    vmem = pl.BlockSpec(memory_space=pltpu.VMEM)
    return pl.pallas_call(
        functools.partial(
            block_kernel, (rows, cols, height, width, chunks, tile_rows, tile_cols, channels, edge)
        ),
        out_shape=jax.ShapeDtypeStruct((2, width, depth), bf16),
        in_specs=[pl.BlockSpec(memory_space=pl.ANY)] * len(operands),
        out_specs=vmem,
        scratch_shapes=[pltpu.VMEM(item.shape, item.dtype) for item in operands[1:]]
        + [
            pltpu.VMEM((tile_rows + 8, wide, channels), bf16),
            pltpu.VMEM((tile_rows + 4, wide, channels), bf16),
            pltpu.VMEM((tile_rows + 4, wide, channels), bf16),
            pltpu.VMEM((tile_rows + 4, wide, channels), bf16),
            pltpu.VMEM((tile_rows, tile_cols, channels), f32),
            pltpu.VMEM((tile_rows, tile_cols, channels), f32),
            kernel_shape,
            kernel_shape,
            pltpu.VMEM((tile_rows, tile_cols, channels), bf16),
            pltpu.VMEM((2, width, channels), bf16),
        ]
        + [exchange] * 6
        + [table] * 4
        + [
            pltpu.VMEM((2, width, lanes), bf16),
            pltpu.VMEM((height, lanes), f32),
            pltpu.VMEM((lanes, depth), bf16),
            pltpu.VMEM((lanes, channels), bf16),
            pltpu.VMEM((lanes, lanes), bf16),
            pltpu.VMEM((2, width, depth), f32),
            pltpu.VMEM((4, tile_cols - tile_cols * 5 // 8, channels), bf16),
            pltpu.VMEM((2, tile_cols - tile_cols * 5 // 8, channels), bf16),
            pltpu.VMEM((2, tile_cols - tile_cols * 5 // 8, channels), bf16),
            pltpu.SemaphoreType.DMA((4, 3)),
            pltpu.SemaphoreType.DMA((len(operands),)),
            pltpu.SemaphoreType.DMA((3, 8)),
            pltpu.SemaphoreType.DMA((3, 8)),
            pltpu.SemaphoreType.DMA((cols,)),
            pltpu.SemaphoreType.DMA((cols,)),
            pltpu.SemaphoreType.DMA((3,)),
            pltpu.SemaphoreType.DMA((3,)),
        ],
        compiler_params=pltpu.CompilerParams(
            collective_id=0, has_side_effects=True, vmem_limit_bytes=56 * 2**20
        ),
        name="block",
    )(*operands)


def solution(mesh):
    in_specs = (
        P("row", "col", None),
        P("row", "col", None),
        P("row", "col"),
        P(),
        P(),
        P(("row", "col"), None, None),
        P(),
        P(),
        P(),
        P(),
    )
    out_specs = P(("row", "col"), None, None)
    return jax.shard_map(shards, mesh=mesh, in_specs=in_specs, out_specs=out_specs, check_vma=False)
```

```python
import functools
import math

import jax
import jax.numpy as jnp
import numpy as np
from jax import lax
from jax.experimental import pallas as pl
from jax.experimental.pallas import tpu as pltpu
from jax.sharding import PartitionSpec as P

MESH = pl.DeviceIdType.MESH
SIDES = [(0, -1), (0, 1), (-1, 0), (1, 0), (-1, -1), (-1, 1), (1, -1), (1, 1)]
UNROLL = 16


def host_tables(length):
    ids = np.arange(length, dtype=np.int64)
    angles = (2.0 * np.pi / length) * ((ids[:, None] * ids[None, :]) % length)
    return (np.cos(angles).astype(jnp.bfloat16), np.sin(angles).astype(jnp.bfloat16))


def dot(left, right):
    return jnp.dot(left, right, preferred_element_type=jnp.float32)


def dot_t(left, right):
    return lax.dot_general(left, right, (((1,), (1,)), ((), ())), preferred_element_type=jnp.float32)


def ids(shape, dim):
    return lax.broadcasted_iota(jnp.int32, shape, dim)


def ones_where(condition):
    return jnp.where(condition, 1.0, 0.0).astype(jnp.bfloat16)


def block_kernel(
    sizes,
    features_any,
    target_any,
    mask_any,
    first_any,
    second_any,
    inputs_any,
    win_any,
    wout_any,
    wlocal_any,
    wmix_any,
    cos_any,
    sin_any,
    out_ref,
    target_ref,
    mask_ref,
    first_ref,
    second_ref,
    inputs_ref,
    win_ref,
    wout_ref,
    wlocal_ref,
    wmix_ref,
    cos_ref,
    sin_ref,
    feat_ext,
    act_ext,
    loss_ext,
    pre_ext,
    slope_first,
    hole_ref,
    first_adj,
    second_adj,
    grad_feat,
    strip_ref,
    spatial_out,
    spatial_in,
    grad_out,
    grad_in,
    back_out,
    back_in,
    col_cos,
    col_sin,
    col_cos_t,
    col_sin_t,
    held,
    slope_mix,
    win_double,
    wout_double,
    wmix_mixed,
    grad_local,
    relay_feat,
    relay_loss,
    relay_pre,
    relay_sems,
    load_sems,
    halo_send,
    halo_recv,
    strip_send,
    strip_recv,
    send_sems,
    recv_sems,
):
    rows, cols, height, width, chunks, tile_rows, tile_cols, channels, edge = sizes
    devices = rows * cols
    half_width = chunks * 64
    lanes = chunks * 128
    freqs = width // 2
    col_factor = 1.0 / math.sqrt(width)
    row_factor = 1.0 / math.sqrt(height)
    my_row = lax.axis_index("row")
    my_col = lax.axis_index("col")
    me = my_row * cols + my_col
    barrier = pltpu.get_barrier_semaphore()

    def each_peer(action, low=0, high=cols):
        for hop in range(low, high):
            col = lax.rem(my_col + hop, cols)
            per_turn = math.gcd(UNROLL, rows)

            def visit(base, k, col=col):
                row = base + (k * 21) % rows
                action(jnp.where(row >= rows, row - rows, row), col)

            def turn(index, carry, visit=visit):
                base = lax.rem(my_row + index * (per_turn * 21), rows)
                for k in range(per_turn):
                    visit(base, k)
                return carry

            if hop == 0:
                for k in range(1, per_turn):
                    visit(my_row, k)
            lax.fori_loop(1 if hop == 0 else 0, rows // per_turn, turn, 0)

    def greet(row, col):
        pl.semaphore_signal(barrier, inc=1, device_id={"row": row, "col": col}, device_id_type=MESH)

    each_peer(greet)

    loads = [
        pltpu.make_async_copy(source, target, load_sems.at[index])
        for index, (source, target) in enumerate(
            [
                (win_any, win_ref),
                (inputs_any, inputs_ref),
                (cos_any, cos_ref),
                (sin_any, sin_ref),
                (first_any, first_ref),
                (second_any, second_ref),
                (features_any, feat_ext.at[pl.ds(4, tile_rows), pl.ds(edge, tile_cols)]),
                (wout_any, wout_ref),
                (wmix_any, wmix_ref),
                (mask_any, mask_ref),
                (target_any, target_ref),
                (wlocal_any, wlocal_ref),
            ]
        )
    ]
    for load in loads:
        load.start()

    def region(side, extent, thick, offset):
        if side < 0:
            return (offset, thick)
        if side > 0:
            return (offset + extent - thick, thick)
        return (offset, extent)

    def landing(side, extent, thick):
        if side < 0:
            return (extent + thick, thick)
        if side > 0:
            return (0, thick)
        return (thick, extent)

    group = 4 if rows % 16 == 0 else 2
    split = tile_cols * 5 // 8
    rest = tile_cols - split
    in_group = lax.rem(my_row, group)
    at_first, at_last = in_group == 0, in_group == group - 1

    def halo_copy(stage, side, source, target, thick, row_offset, col_offset, part=False):
        index = SIDES.index(side)
        source_rows = region(side[0], tile_rows, thick, row_offset)
        source_cols = region(side[1], tile_cols, edge, col_offset)
        target_rows = landing(side[0], tile_rows, thick)
        target_cols = landing(side[1], tile_cols, edge)
        if part:
            source_cols, target_cols = (col_offset, split), (edge, split)
        return pltpu.make_async_remote_copy(
            src_ref=source.at[pl.ds(*source_rows), pl.ds(*source_cols)],
            dst_ref=target.at[pl.ds(*target_rows), pl.ds(*target_cols)],
            send_sem=halo_send.at[stage, index],
            recv_sem=halo_recv.at[stage, index],
            device_id={
                "row": lax.rem(my_row + side[0] + rows, rows),
                "col": lax.rem(my_col + side[1] + cols, cols),
            },
            device_id_type=MESH,
        )

    def exists(side, way):
        row, col = my_row + way * side[0], my_col + way * side[1]
        return (row >= 0) & (row < rows) & (col >= 0) & (col < cols)

    class Exchange:
        def __init__(self, stage, source, target, thick, row_offset, col_offset, buffer):
            common = (source, target, thick, row_offset, col_offset)
            self.whole = [halo_copy(stage, side, *common) for side in SIDES]
            self.part = {index: halo_copy(stage, SIDES[index], *common, part=True) for index in (2, 3)}

            def hop(row_start, distance):
                return pltpu.make_async_remote_copy(
                    src_ref=source.at[pl.ds(row_start, thick), pl.ds(col_offset + split, rest)],
                    dst_ref=buffer,
                    send_sem=relay_sems.at[0, stage],
                    recv_sem=relay_sems.at[1, stage],
                    device_id={"row": lax.rem(my_row + distance + rows, rows), "col": my_col},
                    device_id_type=MESH,
                )

            def onward(row_start, distance):
                return pltpu.make_async_remote_copy(
                    src_ref=buffer,
                    dst_ref=target.at[pl.ds(row_start, thick), pl.ds(edge + split, rest)],
                    send_sem=relay_sems.at[2, stage],
                    recv_sem=relay_sems.at[3, stage],
                    device_id={"row": lax.rem(my_row + distance + rows, rows), "col": my_col},
                    device_id_type=MESH,
                )

            back, ahead = my_row >= group, my_row + group < rows
            up = hop(row_offset, group - 1)
            down = hop(row_offset + tile_rows - thick, 1 - group)
            self.hops = [(at_first & back, up), (at_last & ahead, down)]
            self.onwards = [
                (at_first & ahead, onward(0, group)),
                (at_last & back, onward(thick + tile_rows, -group)),
            ]
            self.finals = [
                (at_first & back, onward(0, group)),
                (at_last & ahead, onward(thick + tile_rows, -group)),
            ]

        def each(self, index, way, action):
            there = exists(SIDES[index], way)
            if index not in (2, 3):
                pl.when(there)(getattr(self.whole[index], action))
                return
            far = at_first if (SIDES[index][0] < 0) == (way > 0) else at_last
            pl.when(there & far)(getattr(self.part[index], action))
            pl.when(there & jnp.logical_not(far))(getattr(self.whole[index], action))

        def begin(self, indices):
            if 2 in indices:
                for there, copy in self.hops:
                    pl.when(there)(copy.start)
            for index in indices:
                self.each(index, 1, "start")

        def relay(self):
            for there, copy in self.onwards:

                @pl.when(there)
                def _(copy=copy):
                    self.hops[0][1].wait_recv()
                    copy.start()

        def receive(self, indices):
            for index in indices:
                self.each(index, -1, "wait_recv")
            if 2 in indices:
                for there, copy in self.finals:
                    pl.when(there)(copy.wait_recv)

        def flush(self):
            for index in range(8):
                self.each(index, 1, "wait_send")
            for there, copy in self.hops + self.onwards:
                pl.when(there)(copy.wait_send)

    def clear_rows(ext, thick):
        @pl.when(my_row == 0)
        def _():
            ext[0:thick] = jnp.zeros_like(ext[0:thick])

        @pl.when(my_row == rows - 1)
        def _():
            ext[thick + tile_rows :] = jnp.zeros_like(ext[thick + tile_rows :])

    def clear_cols(ext):
        @pl.when(my_col == 0)
        def _():
            ext[:, 0:edge] = jnp.zeros_like(ext[:, 0:edge])

        @pl.when(my_col == cols - 1)
        def _():
            ext[:, edge + tile_cols :] = jnp.zeros_like(ext[:, edge + tile_cols :])

    def conv_rows(ext, pieces, first_col, count, kernel):
        results = []
        for start, n in pieces:
            for row in range(start, start + n, 2):
                taps = [
                    ext[row + 2 * a : row + 2 * a + 2, first_col + 2 * b : first_col + 2 * b + count, :]
                    for a in range(3)
                    for b in range(3)
                ]
                joint = jnp.concatenate([tap.reshape(2 * count, channels) for tap in taps], axis=1)
                results.append((row, dot(joint, kernel[...]).reshape(2, count, channels)))
        return results

    for ext, thick in ((feat_ext, 4), (loss_ext, 2), (pre_ext, 2)):
        clear_rows(ext, thick)
        clear_cols(ext)

    even_row = ids((2 * freqs, 128), 0) % 2 == 0
    low_lane = ids((2 * freqs, 128), 1) < 64

    def column_forward(target):
        for j in range(chunks):
            piece = slice(j * 128, (j + 1) * 128)
            both = jnp.concatenate([held[0, :, piece], held[1, :, piece]], axis=1)
            cosine = dot(col_cos[...], both)
            sine = dot(col_sin[...], both)
            first = jnp.where(low_lane, cosine[:, :128], sine[:, :128])
            second = jnp.where(low_lane, cosine[:, 128:], sine[:, 128:])
            mixed_rows = (jnp.where(even_row, first, second) * col_factor).astype(jnp.bfloat16)
            target[j] = mixed_rows.reshape(freqs, 2, 128)

    def messages(source, target, index, low=0, high=cols):
        def send(row, col):
            pltpu.make_async_remote_copy(
                src_ref=source.at[:, row * cols + col],
                dst_ref=target.at[:, me],
                send_sem=send_sems.at[index],
                recv_sem=recv_sems.at[index],
                device_id={"row": row, "col": col},
                device_id_type=MESH,
            ).start()

        each_peer(send, low, high)
        if low == 0:
            pltpu.make_async_copy(source.at[:, me], target.at[:, me], recv_sems.at[index]).start()

    def arrived(target, index):
        pltpu.make_async_copy(target, target, recv_sems.at[index]).wait()

    def sent(source, index):
        rest = source.at[:, pl.ds(0, devices - 1)]
        pltpu.make_async_copy(rest, rest, send_sems.at[index]).wait()

    def row_transform(signal, way):
        sign = jnp.where(ids((height, 128), 1) < 64, way, -way)
        cosine = dot(cos_ref[...], signal)
        sine = dot(sin_ref[...], signal)
        results = []
        for j in range(chunks):
            piece = slice(j * 128, (j + 1) * 128)
            results.append((cosine[:, piece] + pltpu.roll(sine[:, piece], 64, 1) * sign) * row_factor)
        return results

    def collected(source):
        return jnp.concatenate([source[j].reshape(height, 128) for j in range(chunks)], axis=1)

    pl.semaphore_wait(barrier, devices - 1)
    features_out = Exchange(0, features_any, feat_ext, 4, 0, 0, relay_feat)
    features_out.begin(range(8))

    loads[0].wait()
    double_t = ones_where(ids((lanes, half_width), 1) == 64 * (ids((lanes, half_width), 0) // 128) + ids((lanes, half_width), 0) % 64)
    win_double[...] = dot(double_t, win_ref[...]).astype(jnp.bfloat16)
    loads[1].wait()
    for i in range(2):
        held[i] = dot_t(inputs_ref[i], win_double[...]).astype(jnp.bfloat16)
    loads[2].wait()
    loads[3].wait()
    pick = ones_where(ids((2 * freqs, freqs), 0) // 2 == ids((2 * freqs, freqs), 1))
    pick_t = ones_where(ids((freqs, 2 * freqs), 1) // 2 == ids((freqs, 2 * freqs), 0))
    alternate = (1 - 2 * (ids((2 * freqs, width), 1) % 2)).astype(jnp.float32)
    alternate_t = (1 - 2 * (ids((width, 2 * freqs), 0) % 2)).astype(jnp.float32)
    col_cos[...] = dot(pick, cos_ref[:freqs, :]).astype(jnp.bfloat16)
    col_sin[...] = jnp.where(ids((2 * freqs, width), 0) < 2, alternate, -dot(pick, sin_ref[:freqs, :])).astype(jnp.bfloat16)
    column_forward(spatial_out)
    loads[4].wait()
    features_out.receive((0, 1))
    features_out.relay()
    loads[6].wait()

    wide = tile_cols + edge
    margin = edge // 2

    def first_conv(start):
        shape = (2, wide, channels)
        for row, pre in conv_rows(feat_ext, [(start, 4)], edge - margin - 2, wide, first_ref):
            gate = jax.nn.sigmoid(pre)
            row_id = my_row * tile_rows - 2 + row + ids(shape, 0)
            col_id = my_col * tile_cols - margin + ids(shape, 1)
            inside = (row_id >= 0) & (row_id < height) & (col_id >= 0) & (col_id < width)
            act = jnp.where(inside, pre * gate, 0.0).astype(jnp.bfloat16)
            act_ext[row : row + 2, edge - margin : edge - margin + wide, :] = act
            if 2 <= row < 2 + tile_rows:
                slope = gate * (1.0 + pre * (1.0 - gate))
                slope_first[row - 2 : row] = slope[:, margin : margin + tile_cols, :]

    first_conv(4)

    loads[5].wait()
    eye = ones_where(ids((channels, channels), 0) == ids((channels, channels), 1))
    for source, target in ((first_ref, first_adj), (second_ref, second_adj)):
        for tap in range(9):
            block = source[(8 - tap) * channels : (9 - tap) * channels, :]
            target[tap * channels : (tap + 1) * channels, :] = dot_t(eye, block).astype(jnp.bfloat16)
    loads[9].wait()
    spot = ids((tile_cols, tile_cols), 0) == ids((tile_cols, tile_cols), 1)
    for p in range(tile_rows):
        line = mask_ref[p : p + 1, :].astype(jnp.float32)
        spread = jnp.where(spot, line, 0.0).astype(jnp.bfloat16)
        hole_ref[p] = 1.0 + 2.0 * dot(spread, jnp.ones((tile_cols, channels), jnp.bfloat16))
    features_out.receive(range(2, 8))
    first_conv(0)
    first_conv(8)

    outer = [(0, 2), (tile_rows - 2, 2)]
    inner = [(2, tile_rows - 4)]

    body = slice(edge, edge + tile_cols)

    def second_conv(pieces):
        for row, pre in conv_rows(act_ext, pieces, edge - 2, tile_cols, second_ref):
            loss = hole_ref[row : row + 2] * (pre - target_ref[row : row + 2].astype(jnp.float32))
            loss_ext[row + 2 : row + 4, body, :] = loss.astype(jnp.bfloat16)

    loads[10].wait()
    loss_out = Exchange(1, loss_ext, loss_ext, 2, 2, edge, relay_loss)
    second_conv(outer)
    loss_out.begin(range(2, 8))
    second_conv(inner)
    loss_out.begin((0, 1))
    messages(spatial_out, spatial_in, 0, 0, 2)
    loss_out.receive((0, 1))
    loss_out.relay()

    def third_conv(pieces):
        for row, value in conv_rows(loss_ext, pieces, edge - 2, tile_cols, second_adj):
            pre_ext[row + 2 : row + 4, body, :] = (value * slope_first[row : row + 2]).astype(jnp.bfloat16)

    third_conv(inner)
    loss_out.receive(range(2, 8))
    pre_out = Exchange(2, pre_ext, pre_ext, 2, 2, edge, relay_pre)
    third_conv(outer)
    pre_out.begin(range(8))
    messages(spatial_out, spatial_in, 0, 2, cols)

    col_cos_t[...] = dot(cos_ref[:, :freqs], pick_t).astype(jnp.bfloat16)
    col_sin_t[...] = jnp.where(ids((width, 2 * freqs), 1) < 2, alternate_t, -dot(sin_ref[:, :freqs], pick_t)).astype(jnp.bfloat16)
    loads[7].wait()
    wout_double[...] = dot(double_t, wout_ref[...]).astype(jnp.bfloat16)

    def place_of(lane):
        return ((lane % 128) // 64) * half_width + 64 * (lane // 128) + lane % 64

    order = ones_where(ids((lanes, lanes), 0) == place_of(ids((lanes, lanes), 1)))
    order_t = ones_where(ids((lanes, lanes), 1) == place_of(ids((lanes, lanes), 0)))
    loads[8].wait()
    partly = dot(order_t, wmix_ref[...]).astype(jnp.bfloat16)
    wmix_mixed[...] = dot(partly, order).astype(jnp.bfloat16)
    loads[11].wait()
    low_half = ids(win_double.shape, 0) % 128 < 64
    win_double[...] = jnp.where(low_half, win_double[...].astype(jnp.float32), 0.0).astype(jnp.bfloat16)
    pre_out.receive((0, 1))
    pre_out.relay()

    def fourth_conv(pieces):
        for row, value in conv_rows(pre_ext, pieces, edge - 2, tile_cols, first_adj):
            grad_feat[row : row + 2] = value.astype(jnp.bfloat16)

    here = pl.ds(pl.multiple_of(my_col * tile_cols, tile_cols), tile_cols)

    def strip_copy(peer_col):
        return pltpu.make_async_remote_copy(
            src_ref=grad_feat.at[pl.ds(2 * peer_col, 2)],
            dst_ref=strip_ref.at[:, here],
            send_sem=strip_send.at[peer_col],
            recv_sem=strip_recv.at[my_col],
            device_id={"row": my_row, "col": peer_col},
            device_id_type=MESH,
        )

    def strip_own():
        return pltpu.make_async_copy(
            grad_feat.at[pl.ds(2 * my_col, 2)], strip_ref.at[:, here], strip_recv.at[my_col]
        )

    def strip_begin(peer_cols):
        for peer_col in peer_cols:
            pl.when(my_col != peer_col)(strip_copy(peer_col).start)
            pl.when(my_col == peer_col)(strip_own().start)

    def strip_receive():
        for peer_col in range(cols):
            part = strip_ref.at[:, pl.ds(peer_col * tile_cols, tile_cols)]
            pltpu.make_async_copy(part, part, strip_recv.at[peer_col]).wait()

    fourth_conv(inner)
    strip_begin(range(1, cols - 1))
    pre_out.receive(range(2, 8))
    fourth_conv(outer)
    strip_begin((0, cols - 1))

    strip_receive()
    for i in range(2):
        held[i] = dot_t(strip_ref[i], wout_double[...]).astype(jnp.bfloat16)
    column_forward(grad_out)
    messages(grad_out, grad_in, 1)

    arrived(spatial_in, 0)
    freq = row_transform(collected(spatial_in), 1.0)
    pre_mix = dot(jnp.concatenate(freq, axis=1).astype(jnp.bfloat16), wmix_mixed[...])
    gate = jax.nn.sigmoid(pre_mix)
    slope_mix[...] = gate * (1.0 + pre_mix * (1.0 - gate))

    arrived(grad_in, 1)
    freq = row_transform(collected(grad_in), 1.0)
    grad_mix = (jnp.concatenate(freq, axis=1) * slope_mix[...]).astype(jnp.bfloat16)
    mixed = dot_t(grad_mix, wmix_mixed[...]).astype(jnp.bfloat16)
    back = row_transform(mixed, -1.0)
    for j in range(chunks):
        back_out[j] = back[j].astype(jnp.bfloat16).reshape(devices, 2, 128)
    messages(back_out, back_in, 2)
    for exchange in (features_out, loss_out, pre_out):
        exchange.flush()
    for peer_col in range(cols):
        pl.when(my_col != peer_col)(strip_copy(peer_col).wait_send)
    sent(spatial_out, 0)
    sent(grad_out, 1)
    for i in range(2):
        grad_local[i] = dot_t(strip_ref[i], wlocal_ref[...])
    arrived(back_in, 2)
    keep = ids((width, 128), 1) < 64
    for j in range(chunks):
        block = back_in[j].reshape(2 * freqs, 128).astype(jnp.float32)
        both = jnp.concatenate([jnp.where(even_row, block, 0.0), jnp.where(even_row, 0.0, block)], axis=1)
        both = both.astype(jnp.bfloat16)
        cosine = dot(col_cos_t[...], both)
        sine = dot(col_sin_t[...], both)
        for i in range(2):
            piece = slice(i * 128, (i + 1) * 128)
            total = (cosine[:, piece] + pltpu.roll(sine[:, piece], 64, 1)) * col_factor
            held[i, :, j * 128 : (j + 1) * 128] = jnp.where(keep, total, 0.0).astype(jnp.bfloat16)
    for i in range(2):
        out_ref[i] = (dot(held[i], win_double[...]) + grad_local[i]).astype(jnp.bfloat16)
    sent(back_out, 2)


def shards(
    features,
    target,
    hole_mask,
    kernel_first,
    kernel_second,
    inputs,
    weight_in,
    weight_out,
    weight_local,
    weight_mix,
):
    rows, cols = lax.axis_size("row"), lax.axis_size("col")
    devices = rows * cols
    tile_rows, tile_cols, channels = features.shape
    width = inputs.shape[1]
    height = inputs.shape[0] * devices
    depth = inputs.shape[2]
    chunks = weight_in.shape[1] // 64
    lanes = chunks * 128
    edge = min(16, tile_cols)
    cos_table, sin_table = host_tables(width)
    wide = tile_cols + 2 * edge
    bf16, f32 = jnp.bfloat16, jnp.float32
    operands = (
        features,
        target,
        hole_mask,
        kernel_first.reshape(9 * channels, channels),
        kernel_second.reshape(9 * channels, channels),
        inputs,
        weight_in.T,
        weight_out,
        weight_local,
        weight_mix,
        jnp.asarray(cos_table),
        jnp.asarray(sin_table),
    )
    exchange = pltpu.VMEM((chunks, devices, 2, 128), bf16)
    table = pltpu.VMEM((width, width), bf16)
    kernel_shape = pltpu.VMEM((9 * channels, channels), bf16)
    vmem = pl.BlockSpec(memory_space=pltpu.VMEM)
    return pl.pallas_call(
        functools.partial(
            block_kernel, (rows, cols, height, width, chunks, tile_rows, tile_cols, channels, edge)
        ),
        out_shape=jax.ShapeDtypeStruct((2, width, depth), bf16),
        in_specs=[pl.BlockSpec(memory_space=pl.ANY)] * len(operands),
        out_specs=vmem,
        scratch_shapes=[pltpu.VMEM(item.shape, item.dtype) for item in operands[1:]]
        + [
            pltpu.VMEM((tile_rows + 8, wide, channels), bf16),
            pltpu.VMEM((tile_rows + 4, wide, channels), bf16),
            pltpu.VMEM((tile_rows + 4, wide, channels), bf16),
            pltpu.VMEM((tile_rows + 4, wide, channels), bf16),
            pltpu.VMEM((tile_rows, tile_cols, channels), f32),
            pltpu.VMEM((tile_rows, tile_cols, channels), f32),
            kernel_shape,
            kernel_shape,
            pltpu.VMEM((tile_rows, tile_cols, channels), bf16),
            pltpu.VMEM((2, width, channels), bf16),
        ]
        + [exchange] * 6
        + [table] * 4
        + [
            pltpu.VMEM((2, width, lanes), bf16),
            pltpu.VMEM((height, lanes), f32),
            pltpu.VMEM((lanes, depth), bf16),
            pltpu.VMEM((lanes, channels), bf16),
            pltpu.VMEM((lanes, lanes), bf16),
            pltpu.VMEM((2, width, depth), f32),
            pltpu.VMEM((4, tile_cols - tile_cols * 5 // 8, channels), bf16),
            pltpu.VMEM((2, tile_cols - tile_cols * 5 // 8, channels), bf16),
            pltpu.VMEM((2, tile_cols - tile_cols * 5 // 8, channels), bf16),
            pltpu.SemaphoreType.DMA((4, 3)),
            pltpu.SemaphoreType.DMA((len(operands),)),
            pltpu.SemaphoreType.DMA((3, 8)),
            pltpu.SemaphoreType.DMA((3, 8)),
            pltpu.SemaphoreType.DMA((cols,)),
            pltpu.SemaphoreType.DMA((cols,)),
            pltpu.SemaphoreType.DMA((3,)),
            pltpu.SemaphoreType.DMA((3,)),
        ],
        compiler_params=pltpu.CompilerParams(
            collective_id=0, has_side_effects=True, vmem_limit_bytes=56 * 2**20
        ),
        name="block",
    )(*operands)


def solution(mesh):
    in_specs = (
        P("row", "col", None),
        P("row", "col", None),
        P("row", "col"),
        P(),
        P(),
        P(("row", "col"), None, None),
        P(),
        P(),
        P(),
        P(),
    )
    out_specs = P(("row", "col"), None, None)
    return jax.shard_map(shards, mesh=mesh, in_specs=in_specs, out_specs=out_specs, check_vma=False)
```

```python
import functools
import math

import jax
import jax.numpy as jnp
import numpy as np
from jax import lax
from jax.experimental import pallas as pl
from jax.experimental.pallas import tpu as pltpu
from jax.sharding import PartitionSpec as P

MESH = pl.DeviceIdType.MESH
SIDES = [(0, -1), (0, 1), (-1, 0), (1, 0), (-1, -1), (-1, 1), (1, -1), (1, 1)]


def host_tables(length):
    ids = np.arange(length, dtype=np.int64)
    angles = (2.0 * np.pi / length) * ((ids[:, None] * ids[None, :]) % length)
    return (np.cos(angles).astype(jnp.bfloat16), np.sin(angles).astype(jnp.bfloat16))


def dot(left, right):
    return jnp.dot(left, right, preferred_element_type=jnp.float32)


def dot_t(left, right):
    return lax.dot_general(left, right, (((1,), (1,)), ((), ())), preferred_element_type=jnp.float32)


def ids(shape, dim):
    return lax.broadcasted_iota(jnp.int32, shape, dim)


def ones_where(condition):
    return jnp.where(condition, 1.0, 0.0).astype(jnp.bfloat16)


def block_kernel(
    sizes,
    features_any,
    target_any,
    mask_any,
    first_any,
    second_any,
    inputs_any,
    win_any,
    wout_any,
    wlocal_any,
    wmix_any,
    cos_any,
    sin_any,
    out_ref,
    target_ref,
    mask_ref,
    first_ref,
    second_ref,
    inputs_ref,
    win_ref,
    wout_ref,
    wlocal_ref,
    wmix_ref,
    cos_ref,
    sin_ref,
    feat_ext,
    act_ext,
    loss_ext,
    pre_ext,
    slope_first,
    hole_ref,
    first_adj,
    second_adj,
    grad_feat,
    strip_ref,
    spatial_out,
    spatial_in,
    grad_out,
    grad_in,
    back_out,
    back_in,
    col_cos,
    col_sin,
    col_cos_t,
    col_sin_t,
    held,
    slope_mix,
    win_double,
    wout_double,
    wmix_mixed,
    grad_local,
    relay_feat,
    relay_loss,
    relay_pre,
    relay_sems,
    load_sems,
    halo_send,
    halo_recv,
    strip_send,
    strip_recv,
    send_sems,
    recv_sems,
):
    rows, cols, height, width, chunks, tile_rows, tile_cols, channels, edge = sizes
    devices = rows * cols
    half_width = chunks * 64
    lanes = chunks * 128
    freqs = width // 2
    col_factor = 1.0 / math.sqrt(width)
    row_factor = 1.0 / math.sqrt(height)
    my_row = lax.axis_index("row")
    my_col = lax.axis_index("col")
    me = my_row * cols + my_col
    barrier = pltpu.get_barrier_semaphore()

    near = min(4, rows)
    mid = min(4, rows // near)
    far = rows // (near * mid)

    def by_distance(count):
        return sorted(range(count), key=lambda step: -min(step, count - step))

    def each_peer(action, low=0, high=cols):
        for step in by_distance(mid):
            for hop in range(low, high):
                col = lax.rem(my_col + hop, cols)
                own = step == 0 and hop == 0

                def visit(base, k, col=col):
                    row = base + k
                    action(jnp.where(row >= rows, row - rows, row), col)

                def turn(index, carry, own=own, step=step, visit=visit):
                    block = index if own else lax.rem(index + far // 2, far)
                    base = lax.rem(my_row + step * near + block * (near * mid), rows)
                    for k in by_distance(near):
                        visit(base, k)
                    return carry

                lax.fori_loop(1 if own else 0, far, turn, 0)
                if own:
                    for k in range(1, near):
                        visit(my_row, k)

    def greet(row, col):
        pl.semaphore_signal(barrier, inc=1, device_id={"row": row, "col": col}, device_id_type=MESH)

    each_peer(greet)

    loads = [
        pltpu.make_async_copy(source, target, load_sems.at[index])
        for index, (source, target) in enumerate(
            [
                (win_any, win_ref),
                (inputs_any, inputs_ref),
                (cos_any, cos_ref),
                (sin_any, sin_ref),
                (first_any, first_ref),
                (second_any, second_ref),
                (features_any, feat_ext.at[pl.ds(4, tile_rows), pl.ds(edge, tile_cols)]),
                (wout_any, wout_ref),
                (wmix_any, wmix_ref),
                (mask_any, mask_ref),
                (target_any, target_ref),
                (wlocal_any, wlocal_ref),
            ]
        )
    ]
    for load in loads:
        load.start()

    def region(side, extent, thick, offset):
        if side < 0:
            return (offset, thick)
        if side > 0:
            return (offset + extent - thick, thick)
        return (offset, extent)

    def landing(side, extent, thick):
        if side < 0:
            return (extent + thick, thick)
        if side > 0:
            return (0, thick)
        return (thick, extent)

    group = 4 if rows % 16 == 0 else 2
    split = tile_cols * 5 // 8
    rest = tile_cols - split
    in_group = lax.rem(my_row, group)
    at_first, at_last = in_group == 0, in_group == group - 1

    def halo_copy(stage, side, source, target, thick, row_offset, col_offset, part=False):
        index = SIDES.index(side)
        source_rows = region(side[0], tile_rows, thick, row_offset)
        source_cols = region(side[1], tile_cols, edge, col_offset)
        target_rows = landing(side[0], tile_rows, thick)
        target_cols = landing(side[1], tile_cols, edge)
        if part:
            source_cols, target_cols = (col_offset, split), (edge, split)
        return pltpu.make_async_remote_copy(
            src_ref=source.at[pl.ds(*source_rows), pl.ds(*source_cols)],
            dst_ref=target.at[pl.ds(*target_rows), pl.ds(*target_cols)],
            send_sem=halo_send.at[stage, index],
            recv_sem=halo_recv.at[stage, index],
            device_id={
                "row": lax.rem(my_row + side[0] + rows, rows),
                "col": lax.rem(my_col + side[1] + cols, cols),
            },
            device_id_type=MESH,
        )

    def exists(side, way):
        row, col = my_row + way * side[0], my_col + way * side[1]
        return (row >= 0) & (row < rows) & (col >= 0) & (col < cols)

    class Exchange:
        def __init__(self, stage, source, target, thick, row_offset, col_offset, buffer):
            common = (source, target, thick, row_offset, col_offset)
            self.whole = [halo_copy(stage, side, *common) for side in SIDES]
            self.part = {index: halo_copy(stage, SIDES[index], *common, part=True) for index in (2, 3)}

            def hop(row_start, distance):
                return pltpu.make_async_remote_copy(
                    src_ref=source.at[pl.ds(row_start, thick), pl.ds(col_offset + split, rest)],
                    dst_ref=buffer,
                    send_sem=relay_sems.at[0, stage],
                    recv_sem=relay_sems.at[1, stage],
                    device_id={"row": lax.rem(my_row + distance + rows, rows), "col": my_col},
                    device_id_type=MESH,
                )

            def onward(row_start, distance):
                return pltpu.make_async_remote_copy(
                    src_ref=buffer,
                    dst_ref=target.at[pl.ds(row_start, thick), pl.ds(edge + split, rest)],
                    send_sem=relay_sems.at[2, stage],
                    recv_sem=relay_sems.at[3, stage],
                    device_id={"row": lax.rem(my_row + distance + rows, rows), "col": my_col},
                    device_id_type=MESH,
                )

            back, ahead = my_row >= group, my_row + group < rows
            up = hop(row_offset, group - 1)
            down = hop(row_offset + tile_rows - thick, 1 - group)
            self.hops = [(at_first & back, up), (at_last & ahead, down)]
            self.onwards = [
                (at_first & ahead, onward(0, group)),
                (at_last & back, onward(thick + tile_rows, -group)),
            ]
            self.finals = [
                (at_first & back, onward(0, group)),
                (at_last & ahead, onward(thick + tile_rows, -group)),
            ]

        def each(self, index, way, action):
            there = exists(SIDES[index], way)
            if index not in (2, 3):
                pl.when(there)(getattr(self.whole[index], action))
                return
            far = at_first if (SIDES[index][0] < 0) == (way > 0) else at_last
            pl.when(there & far)(getattr(self.part[index], action))
            pl.when(there & jnp.logical_not(far))(getattr(self.whole[index], action))

        def begin(self, indices):
            if 2 in indices:
                for there, copy in self.hops:
                    pl.when(there)(copy.start)
            for index in indices:
                self.each(index, 1, "start")

        def relay(self):
            for there, copy in self.onwards:

                @pl.when(there)
                def _(copy=copy):
                    self.hops[0][1].wait_recv()
                    copy.start()

        def receive(self, indices):
            for index in indices:
                self.each(index, -1, "wait_recv")
            if 2 in indices:
                for there, copy in self.finals:
                    pl.when(there)(copy.wait_recv)

        def flush(self):
            for index in range(8):
                self.each(index, 1, "wait_send")
            for there, copy in self.hops + self.onwards:
                pl.when(there)(copy.wait_send)

    def clear_rows(ext, thick):
        @pl.when(my_row == 0)
        def _():
            ext[0:thick] = jnp.zeros_like(ext[0:thick])

        @pl.when(my_row == rows - 1)
        def _():
            ext[thick + tile_rows :] = jnp.zeros_like(ext[thick + tile_rows :])

    def clear_cols(ext):
        @pl.when(my_col == 0)
        def _():
            ext[:, 0:edge] = jnp.zeros_like(ext[:, 0:edge])

        @pl.when(my_col == cols - 1)
        def _():
            ext[:, edge + tile_cols :] = jnp.zeros_like(ext[:, edge + tile_cols :])

    def conv_rows(ext, pieces, first_col, count, kernel):
        results = []
        for start, n in pieces:
            for row in range(start, start + n, 2):
                taps = [
                    ext[row + 2 * a : row + 2 * a + 2, first_col + 2 * b : first_col + 2 * b + count, :]
                    for a in range(3)
                    for b in range(3)
                ]
                joint = jnp.concatenate([tap.reshape(2 * count, channels) for tap in taps], axis=1)
                results.append((row, dot(joint, kernel[...]).reshape(2, count, channels)))
        return results

    for ext, thick in ((feat_ext, 4), (loss_ext, 2), (pre_ext, 2)):
        clear_rows(ext, thick)
        clear_cols(ext)

    even_row = ids((2 * freqs, 128), 0) % 2 == 0
    low_lane = ids((2 * freqs, 128), 1) < 64

    def column_forward(target):
        for j in range(chunks):
            piece = slice(j * 128, (j + 1) * 128)
            both = jnp.concatenate([held[0, :, piece], held[1, :, piece]], axis=1)
            cosine = dot(col_cos[...], both)
            sine = dot(col_sin[...], both)
            first = jnp.where(low_lane, cosine[:, :128], sine[:, :128])
            second = jnp.where(low_lane, cosine[:, 128:], sine[:, 128:])
            mixed_rows = (jnp.where(even_row, first, second) * col_factor).astype(jnp.bfloat16)
            target[j] = mixed_rows.reshape(freqs, 2, 128)

    def messages(source, target, index, low=0, high=cols):
        def send(row, col):
            pltpu.make_async_remote_copy(
                src_ref=source.at[:, row * cols + col],
                dst_ref=target.at[:, me],
                send_sem=send_sems.at[index],
                recv_sem=recv_sems.at[index],
                device_id={"row": row, "col": col},
                device_id_type=MESH,
            ).start()

        each_peer(send, low, high)
        if low == 0:
            pltpu.make_async_copy(source.at[:, me], target.at[:, me], recv_sems.at[index]).start()

    def arrived(target, index):
        pltpu.make_async_copy(target, target, recv_sems.at[index]).wait()

    def sent(source, index):
        rest = source.at[:, pl.ds(0, devices - 1)]
        pltpu.make_async_copy(rest, rest, send_sems.at[index]).wait()

    def row_transform(signal, way):
        sign = jnp.where(ids((height, 128), 1) < 64, way, -way)
        cosine = dot(cos_ref[...], signal)
        sine = dot(sin_ref[...], signal)
        results = []
        for j in range(chunks):
            piece = slice(j * 128, (j + 1) * 128)
            results.append((cosine[:, piece] + pltpu.roll(sine[:, piece], 64, 1) * sign) * row_factor)
        return results

    def collected(source):
        return jnp.concatenate([source[j].reshape(height, 128) for j in range(chunks)], axis=1)

    pl.semaphore_wait(barrier, devices - 1)
    features_out = Exchange(0, features_any, feat_ext, 4, 0, 0, relay_feat)
    features_out.begin(range(8))

    loads[0].wait()
    double_t = ones_where(ids((lanes, half_width), 1) == 64 * (ids((lanes, half_width), 0) // 128) + ids((lanes, half_width), 0) % 64)
    win_double[...] = dot(double_t, win_ref[...]).astype(jnp.bfloat16)
    loads[1].wait()
    for i in range(2):
        held[i] = dot_t(inputs_ref[i], win_double[...]).astype(jnp.bfloat16)
    loads[2].wait()
    loads[3].wait()
    pick = ones_where(ids((2 * freqs, freqs), 0) // 2 == ids((2 * freqs, freqs), 1))
    pick_t = ones_where(ids((freqs, 2 * freqs), 1) // 2 == ids((freqs, 2 * freqs), 0))
    alternate = (1 - 2 * (ids((2 * freqs, width), 1) % 2)).astype(jnp.float32)
    alternate_t = (1 - 2 * (ids((width, 2 * freqs), 0) % 2)).astype(jnp.float32)
    col_cos[...] = dot(pick, cos_ref[:freqs, :]).astype(jnp.bfloat16)
    col_sin[...] = jnp.where(ids((2 * freqs, width), 0) < 2, alternate, -dot(pick, sin_ref[:freqs, :])).astype(jnp.bfloat16)
    column_forward(spatial_out)
    loads[4].wait()
    features_out.receive((0, 1))
    features_out.relay()
    loads[6].wait()

    wide = tile_cols + edge
    margin = edge // 2

    def first_conv(start):
        shape = (2, wide, channels)
        for row, pre in conv_rows(feat_ext, [(start, 4)], edge - margin - 2, wide, first_ref):
            gate = jax.nn.sigmoid(pre)
            row_id = my_row * tile_rows - 2 + row + ids(shape, 0)
            col_id = my_col * tile_cols - margin + ids(shape, 1)
            inside = (row_id >= 0) & (row_id < height) & (col_id >= 0) & (col_id < width)
            act = jnp.where(inside, pre * gate, 0.0).astype(jnp.bfloat16)
            act_ext[row : row + 2, edge - margin : edge - margin + wide, :] = act
            if 2 <= row < 2 + tile_rows:
                slope = gate * (1.0 + pre * (1.0 - gate))
                slope_first[row - 2 : row] = slope[:, margin : margin + tile_cols, :]

    first_conv(4)

    loads[5].wait()
    eye = ones_where(ids((channels, channels), 0) == ids((channels, channels), 1))
    for source, target in ((first_ref, first_adj), (second_ref, second_adj)):
        for tap in range(9):
            block = source[(8 - tap) * channels : (9 - tap) * channels, :]
            target[tap * channels : (tap + 1) * channels, :] = dot_t(eye, block).astype(jnp.bfloat16)
    loads[9].wait()
    spot = ids((tile_cols, tile_cols), 0) == ids((tile_cols, tile_cols), 1)
    for p in range(tile_rows):
        line = mask_ref[p : p + 1, :].astype(jnp.float32)
        spread = jnp.where(spot, line, 0.0).astype(jnp.bfloat16)
        hole_ref[p] = 1.0 + 2.0 * dot(spread, jnp.ones((tile_cols, channels), jnp.bfloat16))
    features_out.receive(range(2, 8))
    first_conv(0)
    first_conv(8)

    outer = [(0, 2), (tile_rows - 2, 2)]
    inner = [(2, tile_rows - 4)]

    body = slice(edge, edge + tile_cols)

    def second_conv(pieces):
        for row, pre in conv_rows(act_ext, pieces, edge - 2, tile_cols, second_ref):
            loss = hole_ref[row : row + 2] * (pre - target_ref[row : row + 2].astype(jnp.float32))
            loss_ext[row + 2 : row + 4, body, :] = loss.astype(jnp.bfloat16)

    loads[10].wait()
    loss_out = Exchange(1, loss_ext, loss_ext, 2, 2, edge, relay_loss)
    second_conv(outer)
    loss_out.begin(range(2, 8))
    second_conv(inner)
    loss_out.begin((0, 1))
    messages(spatial_out, spatial_in, 0, 0, 2)
    loss_out.receive((0, 1))
    loss_out.relay()

    def third_conv(pieces):
        for row, value in conv_rows(loss_ext, pieces, edge - 2, tile_cols, second_adj):
            pre_ext[row + 2 : row + 4, body, :] = (value * slope_first[row : row + 2]).astype(jnp.bfloat16)

    third_conv(inner)
    loss_out.receive(range(2, 8))
    pre_out = Exchange(2, pre_ext, pre_ext, 2, 2, edge, relay_pre)
    third_conv(outer)
    pre_out.begin(range(8))
    messages(spatial_out, spatial_in, 0, 2, cols)

    col_cos_t[...] = dot(cos_ref[:, :freqs], pick_t).astype(jnp.bfloat16)
    col_sin_t[...] = jnp.where(ids((width, 2 * freqs), 1) < 2, alternate_t, -dot(sin_ref[:, :freqs], pick_t)).astype(jnp.bfloat16)
    loads[7].wait()
    wout_double[...] = dot(double_t, wout_ref[...]).astype(jnp.bfloat16)

    def place_of(lane):
        return ((lane % 128) // 64) * half_width + 64 * (lane // 128) + lane % 64

    order = ones_where(ids((lanes, lanes), 0) == place_of(ids((lanes, lanes), 1)))
    order_t = ones_where(ids((lanes, lanes), 1) == place_of(ids((lanes, lanes), 0)))
    loads[8].wait()
    partly = dot(order_t, wmix_ref[...]).astype(jnp.bfloat16)
    wmix_mixed[...] = dot(partly, order).astype(jnp.bfloat16)
    loads[11].wait()
    low_half = ids(win_double.shape, 0) % 128 < 64
    win_double[...] = jnp.where(low_half, win_double[...].astype(jnp.float32), 0.0).astype(jnp.bfloat16)
    pre_out.receive((0, 1))
    pre_out.relay()

    def fourth_conv(pieces):
        for row, value in conv_rows(pre_ext, pieces, edge - 2, tile_cols, first_adj):
            grad_feat[row : row + 2] = value.astype(jnp.bfloat16)

    here = pl.ds(pl.multiple_of(my_col * tile_cols, tile_cols), tile_cols)

    def strip_copy(peer_col):
        return pltpu.make_async_remote_copy(
            src_ref=grad_feat.at[pl.ds(2 * peer_col, 2)],
            dst_ref=strip_ref.at[:, here],
            send_sem=strip_send.at[peer_col],
            recv_sem=strip_recv.at[my_col],
            device_id={"row": my_row, "col": peer_col},
            device_id_type=MESH,
        )

    def strip_own():
        return pltpu.make_async_copy(
            grad_feat.at[pl.ds(2 * my_col, 2)], strip_ref.at[:, here], strip_recv.at[my_col]
        )

    def strip_begin(peer_cols):
        for peer_col in peer_cols:
            pl.when(my_col != peer_col)(strip_copy(peer_col).start)
            pl.when(my_col == peer_col)(strip_own().start)

    def strip_receive():
        for peer_col in range(cols):
            part = strip_ref.at[:, pl.ds(peer_col * tile_cols, tile_cols)]
            pltpu.make_async_copy(part, part, strip_recv.at[peer_col]).wait()

    fourth_conv(inner)
    strip_begin(range(1, cols - 1))
    pre_out.receive(range(2, 8))
    fourth_conv(outer)
    strip_begin((0, cols - 1))

    strip_receive()
    for i in range(2):
        held[i] = dot_t(strip_ref[i], wout_double[...]).astype(jnp.bfloat16)
    column_forward(grad_out)
    messages(grad_out, grad_in, 1)

    arrived(spatial_in, 0)
    freq = row_transform(collected(spatial_in), 1.0)
    pre_mix = dot(jnp.concatenate(freq, axis=1).astype(jnp.bfloat16), wmix_mixed[...])
    gate = jax.nn.sigmoid(pre_mix)
    slope_mix[...] = gate * (1.0 + pre_mix * (1.0 - gate))

    arrived(grad_in, 1)
    freq = row_transform(collected(grad_in), 1.0)
    grad_mix = (jnp.concatenate(freq, axis=1) * slope_mix[...]).astype(jnp.bfloat16)
    mixed = dot_t(grad_mix, wmix_mixed[...]).astype(jnp.bfloat16)
    back = row_transform(mixed, -1.0)
    for j in range(chunks):
        back_out[j] = back[j].astype(jnp.bfloat16).reshape(devices, 2, 128)
    messages(back_out, back_in, 2)
    for exchange in (features_out, loss_out, pre_out):
        exchange.flush()
    for peer_col in range(cols):
        pl.when(my_col != peer_col)(strip_copy(peer_col).wait_send)
    sent(spatial_out, 0)
    sent(grad_out, 1)
    for i in range(2):
        grad_local[i] = dot_t(strip_ref[i], wlocal_ref[...])
    arrived(back_in, 2)
    keep = ids((width, 128), 1) < 64
    for j in range(chunks):
        block = back_in[j].reshape(2 * freqs, 128).astype(jnp.float32)
        both = jnp.concatenate([jnp.where(even_row, block, 0.0), jnp.where(even_row, 0.0, block)], axis=1)
        both = both.astype(jnp.bfloat16)
        cosine = dot(col_cos_t[...], both)
        sine = dot(col_sin_t[...], both)
        for i in range(2):
            piece = slice(i * 128, (i + 1) * 128)
            total = (cosine[:, piece] + pltpu.roll(sine[:, piece], 64, 1)) * col_factor
            held[i, :, j * 128 : (j + 1) * 128] = jnp.where(keep, total, 0.0).astype(jnp.bfloat16)
    for i in range(2):
        out_ref[i] = (dot(held[i], win_double[...]) + grad_local[i]).astype(jnp.bfloat16)
    sent(back_out, 2)


def shards(
    features,
    target,
    hole_mask,
    kernel_first,
    kernel_second,
    inputs,
    weight_in,
    weight_out,
    weight_local,
    weight_mix,
):
    rows, cols = lax.axis_size("row"), lax.axis_size("col")
    devices = rows * cols
    tile_rows, tile_cols, channels = features.shape
    width = inputs.shape[1]
    height = inputs.shape[0] * devices
    depth = inputs.shape[2]
    chunks = weight_in.shape[1] // 64
    lanes = chunks * 128
    edge = min(16, tile_cols)
    cos_table, sin_table = host_tables(width)
    wide = tile_cols + 2 * edge
    bf16, f32 = jnp.bfloat16, jnp.float32
    operands = (
        features,
        target,
        hole_mask,
        kernel_first.reshape(9 * channels, channels),
        kernel_second.reshape(9 * channels, channels),
        inputs,
        weight_in.T,
        weight_out,
        weight_local,
        weight_mix,
        jnp.asarray(cos_table),
        jnp.asarray(sin_table),
    )
    exchange = pltpu.VMEM((chunks, devices, 2, 128), bf16)
    table = pltpu.VMEM((width, width), bf16)
    kernel_shape = pltpu.VMEM((9 * channels, channels), bf16)
    vmem = pl.BlockSpec(memory_space=pltpu.VMEM)
    return pl.pallas_call(
        functools.partial(
            block_kernel, (rows, cols, height, width, chunks, tile_rows, tile_cols, channels, edge)
        ),
        out_shape=jax.ShapeDtypeStruct((2, width, depth), bf16),
        in_specs=[pl.BlockSpec(memory_space=pl.ANY)] * len(operands),
        out_specs=vmem,
        scratch_shapes=[pltpu.VMEM(item.shape, item.dtype) for item in operands[1:]]
        + [
            pltpu.VMEM((tile_rows + 8, wide, channels), bf16),
            pltpu.VMEM((tile_rows + 4, wide, channels), bf16),
            pltpu.VMEM((tile_rows + 4, wide, channels), bf16),
            pltpu.VMEM((tile_rows + 4, wide, channels), bf16),
            pltpu.VMEM((tile_rows, tile_cols, channels), f32),
            pltpu.VMEM((tile_rows, tile_cols, channels), f32),
            kernel_shape,
            kernel_shape,
            pltpu.VMEM((tile_rows, tile_cols, channels), bf16),
            pltpu.VMEM((2, width, channels), bf16),
        ]
        + [exchange] * 6
        + [table] * 4
        + [
            pltpu.VMEM((2, width, lanes), bf16),
            pltpu.VMEM((height, lanes), f32),
            pltpu.VMEM((lanes, depth), bf16),
            pltpu.VMEM((lanes, channels), bf16),
            pltpu.VMEM((lanes, lanes), bf16),
            pltpu.VMEM((2, width, depth), f32),
            pltpu.VMEM((4, tile_cols - tile_cols * 5 // 8, channels), bf16),
            pltpu.VMEM((2, tile_cols - tile_cols * 5 // 8, channels), bf16),
            pltpu.VMEM((2, tile_cols - tile_cols * 5 // 8, channels), bf16),
            pltpu.SemaphoreType.DMA((4, 3)),
            pltpu.SemaphoreType.DMA((len(operands),)),
            pltpu.SemaphoreType.DMA((3, 8)),
            pltpu.SemaphoreType.DMA((3, 8)),
            pltpu.SemaphoreType.DMA((cols,)),
            pltpu.SemaphoreType.DMA((cols,)),
            pltpu.SemaphoreType.DMA((3,)),
            pltpu.SemaphoreType.DMA((3,)),
        ],
        compiler_params=pltpu.CompilerParams(
            collective_id=0, has_side_effects=True, vmem_limit_bytes=56 * 2**20
        ),
        name="block",
    )(*operands)


def solution(mesh):
    in_specs = (
        P("row", "col", None),
        P("row", "col", None),
        P("row", "col"),
        P(),
        P(),
        P(("row", "col"), None, None),
        P(),
        P(),
        P(),
        P(),
    )
    out_specs = P(("row", "col"), None, None)
    return jax.shard_map(shards, mesh=mesh, in_specs=in_specs, out_specs=out_specs, check_vma=False)
```
